32 devices in a mesh: dp: 2 (over x), cols: 16 (over z, y, core).
Axes of the slice: x: 2, y: 2, z: 4, core: 2. Of those that a mesh axis runs over, the one named last changes fastest.
Arguments:
- tokens: bfloat16 [512, 4096], P(('dp', 'cols')), may hold values from -6 to 6
- cotangent: bfloat16 [512, 4096], P(('dp', 'cols')), may hold values from -6 to 6
- block_weights: bfloat16 [4096, 128, 128], P('cols'), may hold values from -0.15625 to 0.15625
- slot_block: int32 [4096], P('cols'), may hold values from 0 to 31
- slot_target: int32 [4096], P('cols'), may hold values from 0 to 23, as said below
- counts: int32 [16], P('cols'), may hold values from 171 to 256, as said below
Outputs:
- input_grad: bfloat16 [512, 4096], P(('dp', 'cols'))
- weight_grad: bfloat16 [4096, 128, 128], P('cols', 'dp')
The draws below stay inside these ranges and needn't reach their ends.
Inputs may be any that keep to these rules, and one draw needn't show every extreme that they name: On each device the live slots name distinct pairs of slot_target and slot_block; slot_target // 8 gives the matrix (0 gate, 1 up, 2 down). `counts`: some device has all 256 slots live.
All inputs are finite; a program needn't handle non-finite values.
Results may differ from the reference program's by a relative error of at most 0.018.
Values may be sent and summed in bfloat16 or wider, within the bound.
A program may use at most 192 MiB of HBM per device.

```python
import jax
import jax.numpy as jnp
from jax import lax

D = 4096
BLK = 128
NDB = 32
CPD = 8
SLOTS = 256
TOKENS = 512
N_DP = 2
N_COLS = 16


def pattern(key):
    base_key = jax.random.fold_in(key, 17)
    device_keys = jax.random.split(base_key, N_COLS)
    pair_total = 3 * CPD * NDB
    chosen = jax.vmap(lambda device_key: jax.random.permutation(device_key, pair_total)[:SLOTS])(device_keys)
    return chosen.reshape(-1).astype(jnp.int32)


def draw_slot_block(key, part):
    return (pattern(key) % NDB).astype(jnp.int32)


def draw_slot_target(key, part):
    return (pattern(key) // NDB).astype(jnp.int32)


def draw_counts(key, part):
    first_key, second_key = jax.random.split(jax.random.fold_in(key, 29))
    totals = jax.random.randint(first_key, (N_COLS,), SLOTS - SLOTS // 3, SLOTS + 1)
    device_pick = jax.random.randint(second_key, (), 0, N_COLS)
    return totals.at[device_pick].set(SLOTS).astype(jnp.int32)


def block_levels(rng, dims, cuts, low, top_value):
    loudness, own = 1.0, jax.random.fold_in(rng, 6)
    for axis_at, parts in cuts:
        steps = jnp.exp(jax.random.uniform(jax.random.fold_in(own, axis_at), (parts,), jnp.float32, low / len(cuts), top_value / len(cuts)))
        loudness = loudness * jnp.repeat(steps, dims[axis_at] // parts).reshape([-1 if axis == axis_at else 1 for axis in range(len(dims))])
    return loudness


def gaussian(own_key, extent, deviation, limit, pieces=(), kind=jnp.bfloat16):
    drawn = deviation * jax.random.normal(own_key, extent, jnp.float32)
    if pieces:
        drawn = drawn * block_levels(own_key, extent, pieces, -0.22, 0.18)
    return jnp.clip(drawn, -limit, limit).astype(kind)


def setup_inputs(seed: int = 0) -> dict:
    streams_of = jax.random.split(jax.random.key(seed), 7)
    tokens = gaussian(streams_of[0], (TOKENS, D), 1.0, 6.0, ((0, 32),))
    cotangent = gaussian(streams_of[1], (TOKENS, D), 1.0, 6.0, ((0, 32),))
    block_weights = gaussian(streams_of[2], (N_COLS * SLOTS, BLK, BLK), (BLK * SLOTS // (3 * CPD)) ** -0.5, 0.15625, ((0, 16),))
    slot_block = draw_slot_block(jax.random.fold_in(streams_of[6], 71), 0)
    slot_target = draw_slot_target(jax.random.fold_in(streams_of[6], 71), 0)
    counts = draw_counts(jax.random.fold_in(streams_of[6], 71), 0)
    return {"tokens": tokens, "cotangent": cotangent, "block_weights": block_weights, "slot_block": slot_block, "slot_target": slot_target, "counts": counts}


def local_pass(tokens_rows, cotangent_rows, weights, slot_blocks, slot_targets, live_count):
    row_count = tokens_rows.shape[0]
    slot_total = weights.shape[0]
    block_width = weights.shape[1]
    block_count = tokens_rows.shape[1] // block_width
    columns = CPD
    live_slot = jnp.arange(slot_total) < live_count
    slot_kind = slot_targets // columns
    places = slot_targets % columns
    select_up = jax.nn.one_hot(slot_targets, 2 * columns, dtype=jnp.float32) * (live_slot & (slot_kind < 2))[:, None].astype(jnp.float32)
    select_down = jax.nn.one_hot(places, columns, dtype=jnp.float32) * (live_slot & (slot_kind == 2))[:, None].astype(jnp.float32)
    block_select = jax.nn.one_hot(slot_blocks, block_count, dtype=jnp.float32)
    wide_weights = weights.astype(jnp.float32)
    tokens_slots = jnp.take(tokens_rows.reshape(row_count, block_count, block_width), slot_blocks, axis=1).astype(jnp.float32)
    cot_slots = jnp.take(cotangent_rows.reshape(row_count, block_count, block_width), slot_blocks, axis=1).astype(jnp.float32)
    products = jnp.einsum('rsk,skj->rsj', tokens_slots, wide_weights)
    gate_up = jnp.einsum('rsj,sc->rcj', products, select_up)
    gate_pre = gate_up[:, :columns]
    up_pre = gate_up[:, columns:]
    sigmoid_gate = jax.nn.sigmoid(gate_pre)
    silu_gate = gate_pre * sigmoid_gate
    hidden = (silu_gate * up_pre).astype(jnp.bfloat16)
    back_products = jnp.einsum('rsj,skj->rsk', cot_slots, wide_weights)
    hidden_grad = jnp.einsum('rsk,sc->rck', back_products, select_down)
    gate_grad = (hidden_grad * up_pre * sigmoid_gate * (1.0 + gate_pre * (1.0 - sigmoid_gate))).astype(jnp.bfloat16)
    up_grad = (hidden_grad * silu_gate).astype(jnp.bfloat16)
    pre_grad = jnp.concatenate([gate_grad, up_grad], axis=1).astype(jnp.float32)
    slot_grad = jnp.einsum('rck,sc->rsk', pre_grad, select_up)
    slot_hidden = jnp.einsum('rck,sc->rsk', hidden.astype(jnp.float32), select_down)
    weight_terms = jnp.einsum('rsk,rsj->skj', tokens_slots, slot_grad) + jnp.einsum('rsk,rsj->skj', slot_hidden, cot_slots)
    input_slots = jnp.einsum('rsj,skj->rsk', slot_grad, wide_weights)
    input_terms = jnp.einsum('rsk,sb->rbk', input_slots, block_select).reshape(row_count, block_count * block_width)
    return weight_terms, input_terms


def reference(tokens, cotangent, block_weights, slot_block, slot_target, counts):
    row_group = tokens.shape[0] // N_DP
    weights = block_weights.reshape(N_COLS, SLOTS, BLK, BLK)
    blocks_table = slot_block.reshape(N_COLS, SLOTS)
    targets_table = slot_target.reshape(N_COLS, SLOTS)
    grad_total = jnp.zeros((N_COLS, SLOTS, BLK, BLK), jnp.float32)
    input_parts = []
    for group_index in range(N_DP):
        tokens_rows = tokens[group_index * row_group:(group_index + 1) * row_group]
        cot_rows = cotangent[group_index * row_group:(group_index + 1) * row_group]

        def device_step(carry, device_items):
            weight_one, block_one, target_one, count_one = device_items
            weight_terms, input_terms = local_pass(tokens_rows, cot_rows, weight_one, block_one, target_one, count_one)
            return carry + input_terms, weight_terms

        start_sum = jnp.zeros((row_group, tokens.shape[1]), jnp.float32)
        input_sum, weight_parts = lax.scan(device_step, start_sum, (weights, blocks_table, targets_table, counts))
        rounded = lax.optimization_barrier(weight_parts.astype(jnp.bfloat16))
        grad_total = grad_total + rounded.astype(jnp.float32)
        input_parts.append(input_sum.astype(jnp.bfloat16))
    input_grad = jnp.concatenate(input_parts, axis=0)
    weight_grad = grad_total.astype(jnp.bfloat16).reshape(N_COLS * SLOTS, BLK, BLK)
    return input_grad, weight_grad
```

```python
import functools

import jax
import jax.numpy as jnp
from jax import lax
from jax.experimental import pallas as pl
from jax.experimental.pallas import tpu as pltpu
from jax.sharding import PartitionSpec as P

SPC = 32


def block_inputs(grad_rows, weights, block_select):
    partial_rows = jnp.einsum(
        "rsj,skj->rsk", grad_rows, weights, preferred_element_type=jnp.float32
    )
    summed = jnp.einsum("rsk,sb->rbk", partial_rows, block_select)
    return summed.reshape(summed.shape[0], summed.shape[1] * summed.shape[2])


def shards(tokens, cotangent, block_weights, slot_block, slot_target, counts):
    slot_total = block_weights.shape[0]
    block_width = block_weights.shape[1]
    columns = slot_total // SPC
    features = tokens.shape[1]
    block_count = features // block_width
    tokens_all, cot_all = (
        lax.all_gather(tokens, "cols", axis=0, tiled=True),
        lax.all_gather(cotangent, "cols", axis=0, tiled=True),
    )
    row_total = tokens_all.shape[0]
    live_slot = jnp.arange(slot_total) < counts[0]
    slot_kind = slot_target // columns
    places = slot_target % columns
    up_mask = (live_slot & (slot_kind < 2))[:, None].astype(jnp.float32)
    down_mask = (live_slot & (slot_kind == 2))[:, None].astype(jnp.float32)
    select_up = jax.nn.one_hot(slot_target, 2 * columns, dtype=jnp.float32) * up_mask
    select_down = jax.nn.one_hot(places, columns, dtype=jnp.float32) * down_mask
    block_select = jax.nn.one_hot(slot_block, block_count, dtype=jnp.float32)
    tokens_slots = jnp.take(
        tokens_all.reshape(row_total, block_count, block_width), slot_block, axis=1
    )
    products = jnp.einsum(
        "rsk,skj->rsj", tokens_slots, block_weights, preferred_element_type=jnp.float32
    )
    gate_up = jnp.einsum("rsj,sc->rcj", products, select_up)
    gate_pre = gate_up[:, :columns]
    up_pre = gate_up[:, columns:]
    sigmoid_gate = jax.nn.sigmoid(gate_pre)
    silu_gate = gate_pre * sigmoid_gate
    hidden = (silu_gate * up_pre).astype(jnp.bfloat16)
    cot_slots = jnp.take(cot_all.reshape(row_total, block_count, block_width), slot_block, axis=1)
    back_products = jnp.einsum(
        "rsj,skj->rsk", cot_slots, block_weights, preferred_element_type=jnp.float32
    )
    hidden_grad = jnp.einsum("rsk,sc->rck", back_products, select_down)
    gate_grad = (
        hidden_grad * up_pre * sigmoid_gate * (1.0 + gate_pre * (1.0 - sigmoid_gate))
    ).astype(jnp.bfloat16)
    up_grad = (hidden_grad * silu_gate).astype(jnp.bfloat16)
    pre_grad = jnp.concatenate([gate_grad, up_grad], axis=1)
    slot_grad = jnp.einsum(
        "rck,sc->rsk", pre_grad, select_up.astype(jnp.bfloat16), preferred_element_type=jnp.float32
    ).astype(jnp.bfloat16)
    slot_hidden = jnp.einsum(
        "rck,sc->rsk", hidden, select_down.astype(jnp.bfloat16), preferred_element_type=jnp.float32
    ).astype(jnp.bfloat16)
    weight_terms = jnp.einsum(
        "rsk,rsj->skj", tokens_slots, slot_grad, preferred_element_type=jnp.float32
    )
    weight_terms = weight_terms + jnp.einsum(
        "rsk,rsj->skj", slot_hidden, cot_slots, preferred_element_type=jnp.float32
    )
    input_terms = block_inputs(slot_grad, block_weights, block_select)
    input_sum = lax.psum_scatter(input_terms, "cols", scatter_dimension=0, tiled=True)
    input_grad = input_sum.astype(jnp.bfloat16)
    weight_sum = lax.psum_scatter(
        weight_terms.astype(jnp.bfloat16), "dp", scatter_dimension=1, tiled=True
    )
    return (input_grad, weight_sum)


MESH = pl.DeviceIdType.MESH
F32 = jnp.float32
BF16 = jnp.bfloat16
NT = (((1,), (1,)), ((), ()))
CHUNKS = 4
GROUP = 4
LANES = 128


def layer_kernel(
    n_cols, count_ref, target_ref, block_ref, tok_ref, cot_ref, w_ref, in_ref, out_ref,
    tok, cot, blocks, wgu, wd, grads, hid, pre, acc, sib_out, sib_in, chip_sum, a2a,
    fin_out, fin_in, lhs, hid_t, table_rows, table_ref,
    w_sem, own_sem, table_sem, out_sem, ring_send, ring_recv, sib_send, sib_recv,
    x_send, x_recv, half_send, half_recv, a2a_send, a2a_recv, fin_send, fin_recv,
):
    chips = n_cols // 2
    steps = chips // 2
    rows = tok_ref.shape[0]
    group_rows = rows * n_cols
    features = tok_ref.shape[1]
    width = blocks.shape[2]
    part = blocks.shape[1]
    n_f = features // width
    hidden = wd.shape[0]
    n_h = hidden // width
    zero_at = blocks.shape[0] - 1
    zero_slot = zero_at
    half = features // 2
    dp = lax.axis_index("dp")
    col = lax.axis_index("cols")
    core = col % 2
    chip = col // 2
    place = jnp.where(chip % 2 == 0, chip // 2, chips - 1 - chip // 2)

    def chip_at(p):
        p = (p + 2 * chips) % chips
        return jnp.where(p < steps, 2 * p, 2 * (chips - 1 - p) + 1)

    right = chip_at(place + 1) * 2 + core
    left = chip_at(place - 1) * 2 + core
    sibling = chip * 2 + 1 - core
    sides = ((tok_ref, tok), (cot_ref, cot))

    owns = [pltpu.make_async_copy(sides[a][0], sides[a][1].at[0, col], own_sem.at[a]) for a in range(2)]
    for own in owns:
        own.start()
    w_copy = pltpu.make_async_copy(w_ref, blocks.at[pl.ds(0, w_ref.shape[0])], w_sem)
    w_copy.start()
    barrier = pltpu.get_barrier_semaphore()
    for r in range(1, chips):
        pl.semaphore_signal(barrier, inc=1, device_id=(dp, ((chip + r) % chips) * 2 + core), device_id_type=MESH)
    pl.semaphore_signal(barrier, inc=1, device_id=(dp, sibling), device_id_type=MESH)
    pl.semaphore_signal(barrier, inc=1, device_id=(1 - dp, col), device_id_type=MESH)
    pl.semaphore_wait(barrier, chips + 1)

    def piece(g, origin, a):
        at = pl.ds((a % 2) * half, half)
        return sides[a // 2][1].at[g, origin * 2 + core, :, at]

    def ring_copy(g, origin, direction, s, a):
        block = piece(g, origin, a)
        return pltpu.make_async_remote_copy(
            src_ref=block, dst_ref=block,
            send_sem=ring_send, recv_sem=ring_recv.at[g * steps + s, direction, a],
            device_id=(dp, right if direction == 0 else left), device_id_type=MESH,
        )

    def ring(g, direction, s, a):
        return ring_copy(g, chip_at(place - s if direction == 0 else place + s), direction, s, a)

    def ring_arrival(g, direction, s, a):
        return ring_copy(g, chip_at(place - 1 - s if direction == 0 else place + 1 + s), direction, s, a)

    def share_copy(g, k, a, lane):
        at = pl.ds((a % 2) * half, half)
        block = sides[a // 2][1].at[g, chip_at(place - k) * 2 + lane, :, at]
        return pltpu.make_async_remote_copy(
            src_ref=block, dst_ref=block,
            send_sem=sib_send, recv_sem=sib_recv.at[g, a // 2],
            device_id=(dp, sibling), device_id_type=MESH,
        )

    def share(g, k, a):
        return share_copy(g, k, a, core)

    def cross(k, a):
        origin = chip_at(place - k)
        return pltpu.make_async_remote_copy(
            src_ref=piece(0, origin, a), dst_ref=piece(1, origin, a),
            send_sem=x_send, recv_sem=x_recv.at[k],
            device_id=(1 - dp, col), device_id_type=MESH,
        )

    def first(g, arr):
        for a in (2 * arr, 2 * arr + 1):
            for direction in range(2):
                ring(g, direction, 0, a).start()
        for a in (2 * arr, 2 * arr + 1):
            share(g, 0, a).start()
            if g == 0:
                cross(0, a).start()

    def pass_on(s, direction, a):
        ring_arrival(0, direction, s, a).wait_recv()

        far = steps - 1 if a % 2 == direction else steps - 2

        @pl.when(s < far)
        def _():
            ring(0, direction, s + 1, a).start()

        k = 1 + s if direction == 0 else chips - 1 - s
        share(0, k, a).start()

        @pl.when(s > 0)
        def _():
            cross(k, a).start()

    def advance(s, arr):
        for direction in range(2):
            pass_on(s, direction, 2 * arr + direction)

        @pl.when(s < steps - 1)
        def _():
            for direction in range(2):
                pass_on(s, direction, 2 * arr + 1 - direction)

    def bulk(ref, send_sem, recv_sem, device):
        return pltpu.make_async_remote_copy(
            src_ref=ref, dst_ref=ref, send_sem=send_sem, recv_sem=recv_sem,
            device_id=device, device_id_type=MESH,
        )

    def all_shared(g, arr):
        bulk(sides[arr][1].at[g, pl.ds(0, chips)], sib_send, sib_recv.at[g, arr], (dp, sibling)).wait_recv()

    def cross_arrival(k):
        bulk(tok.at[1, pl.ds(0, 2)], x_send, x_recv.at[k], (1 - dp, col)).wait_recv()

    def crossed(k):
        cross_arrival(k)
        for a in range(4):
            share(1, k, a).start()

    for own in owns:
        own.wait()
    first(0, 0)

    slot_place = target_ref[...] * n_f + block_ref[...]
    number = lax.broadcasted_iota(jnp.int32, slot_place.shape, 0) * LANES + lax.broadcasted_iota(
        jnp.int32, slot_place.shape, 1
    )
    slot_place = jnp.where(number < count_ref[0], slot_place, -1)
    lane = lax.broadcasted_iota(jnp.int32, (LANES, LANES), 1)
    in_row = lax.broadcasted_iota(jnp.int32, (LANES, LANES), 0)
    columns = [
        jnp.broadcast_to(slot_place[j:j + 1], (LANES, LANES)).T for j in range(slot_place.shape[0])
    ]
    for t in range(zero_slot // LANES):
        row = jnp.zeros((1, LANES), jnp.int32)
        for j, column in enumerate(columns):
            hit = column == lane + t * LANES
            row = row + jnp.sum(
                jnp.where(hit, in_row + (j * LANES - zero_slot), 0), axis=0, keepdims=True
            )
        table_rows[t:t + 1, :] = row + zero_slot
    table_copy = pltpu.make_async_copy(table_rows, table_ref, table_sem)
    table_copy.start()
    blocks[zero_at] = jnp.zeros((part, width), BF16)
    w_copy.wait()
    table_copy.wait()

    pieces = width // part

    def spread(h, f):
        at = pl.multiple_of(f * width, width)
        hid_at = pl.multiple_of(h * width, width)
        for k in range(3):
            entry = (k * n_h + h) * n_f + f
            index = table_ref[entry // LANES, entry % LANES]
            for piece in range(pieces):
                value = blocks[jnp.minimum(index * pieces + piece, zero_at)]
                if k < 2:
                    wgu[pl.ds(pl.multiple_of(at + piece * part, part), part),
                        pl.ds(pl.multiple_of(k * hidden + hid_at, width), width)] = value
                else:
                    wd[pl.ds(pl.multiple_of(hid_at + piece * part, part), part), pl.ds(at, width)] = value

    per_step = n_h // steps

    @pl.loop(0, steps)
    def _(s):
        @pl.loop(0, n_f)
        def _(f):
            for j in range(per_step):
                spread(s * per_step + j, f)

        advance(s, 0)

        @pl.when(s == steps // 2 - 1)
        def _():
            first(0, 1)

    all_shared(0, 0)
    span = hidden // steps

    def before(g, n):
        at = pl.multiple_of(n * span, span)
        x = tok[g].reshape(group_rows, features)
        gate = jnp.dot(x, wgu[:, pl.ds(at, span)], preferred_element_type=F32)
        up = jnp.dot(x, wgu[:, pl.ds(pl.multiple_of(hidden + at, span), span)], preferred_element_type=F32)
        return gate, up

    def after(g, n, gate, up):
        at = pl.multiple_of(n * span, span)
        back = lax.dot_general(
            cot[g].reshape(group_rows, features), wd[pl.ds(at, span), :], NT, preferred_element_type=F32
        )
        sig = jax.nn.sigmoid(gate)
        silu = gate * sig
        hid[g, :, pl.ds(at, span)] = (silu * up).astype(BF16)
        grads[g, :, pl.ds(at, span)] = (back * up * sig * (1.0 + gate * (1.0 - sig))).astype(BF16)
        grads[g, :, pl.ds(pl.multiple_of(hidden + at, span), span)] = (back * silu).astype(BF16)

    @pl.loop(0, steps)
    def _(s):
        gate, up = before(0, s)
        pre[s, 0] = gate
        pre[s, 1] = up
        advance(s, 1)

    cross_arrival(0)
    first(1, 0)
    first(1, 1)
    all_shared(0, 1)

    @pl.loop(0, steps)
    def _(s):
        after(0, s, pre[s, 0], pre[s, 1])

    crossed(2)
    crossed(chips - 2)

    chunk = half // CHUNKS
    chip_rows = group_rows // chips

    def terms(at):
        return lax.dot_general(grads[0], wgu[pl.ds(at, chunk), :], NT, preferred_element_type=F32)

    def to_sibling(i):
        return pltpu.make_async_remote_copy(
            src_ref=sib_out.at[i], dst_ref=sib_in.at[i], send_sem=half_send, recv_sem=half_recv.at[i],
            device_id=(dp, sibling), device_id_type=MESH,
        )

    def spread_sum(r, i):
        other = (chip + r) % chips
        return pltpu.make_async_remote_copy(
            src_ref=chip_sum.at[i, other], dst_ref=a2a.at[i, r],
            send_sem=a2a_send, recv_sem=a2a_recv.at[i],
            device_id=(dp, other * 2 + core), device_id_type=MESH,
        )

    def pair_sum(i):
        to_sibling(i).wait_recv()

        @pl.loop(0, chips)
        def _(c):
            at = pl.ds(pl.multiple_of(c * chip_rows, chip_rows), chip_rows)
            total = acc[i, at, :] + sib_in[i, at, :].astype(F32)
            acc[i, at, :] = total
            chip_sum[i, c] = total.astype(BF16)

        @pl.loop(1, chips)
        def _(r):
            spread_sum(r, i).start()

    @pl.loop(0, CHUNKS)
    def _(i):
        at = pl.multiple_of(i * chunk, chunk)
        sib_out[i] = terms(pl.multiple_of((1 - core) * half + at, chunk)).astype(BF16)
        to_sibling(i).start()
        acc[i] = terms(pl.multiple_of(core * half + at, chunk))

        @pl.when(i > 0)
        def _():
            pair_sum(i - 1)

    pair_sum(CHUNKS - 1)

    for direction in range(2):
        for a in range(4):
            ring_arrival(1, direction, 0, a).wait_recv()
            share(1, 1 if direction == 0 else chips - 1, a).start()

    @pl.loop(3, chips - 2)
    def _(k):
        crossed(k)

    all_shared(1, 0)
    all_shared(1, 1)

    @pl.loop(0, steps)
    def _(s):
        gate, up = before(1, s)
        after(1, s, gate, up)

    def take_part(block):
        out = block[:part]
        for i in range(1, width // part):
            out = jnp.where(dp == i, block[i * part:(i + 1) * part], out)
        return out

    for g in range(2):
        for h in range(n_h):
            hid_t[pl.ds(h * part, part), pl.ds(g * group_rows, group_rows)] = take_part(
                hid[g, :, pl.ds(h * width, width)].T
            )
    four = GROUP
    per_piece = 3 * n_h * four
    cuts = 4

    def send_out(i, c):
        at = pl.ds(i * per_piece + c * (per_piece // cuts), per_piece // cuts)
        return pltpu.make_async_copy(blocks.at[at], out_ref.at[at], out_sem)

    zero_out = pltpu.make_async_copy(blocks.at[zero_at], out_ref.at[zero_at], table_sem)
    zero_out.start()

    @pl.loop(0, n_f // four)
    def _(i):
        at = pl.multiple_of(i * four * width, four * width)
        for g in range(2):
            for b in range(four):
                piece = tok[g, :, :, pl.ds(pl.multiple_of(at + b * width, width), width)]
                lhs[pl.ds(b * part, part), pl.ds(g * group_rows, group_rows)] = take_part(
                    piece.reshape(group_rows, width).T
                )
        base = i * per_piece
        for n in range(2 * n_h // 4):
            cut = slice(n * 4 * width, (n + 1) * 4 * width)
            out = jnp.dot(
                lhs[...], grads[:, :, cut].reshape(2 * group_rows, 4 * width), preferred_element_type=F32
            ).astype(BF16)
            for h in range(4):
                for b in range(four):
                    blocks[base + (n * 4 + h) * four + b] = out[
                        b * part:(b + 1) * part, h * width:(h + 1) * width
                    ]
        c = cot[:, :, :, pl.ds(at, four * width)].reshape(2 * group_rows, four * width)
        out = jnp.dot(hid_t[...], c, preferred_element_type=F32).astype(BF16)
        for h in range(n_h):
            for b in range(four):
                blocks[base + (2 * n_h + h) * four + b] = out[
                    h * part:(h + 1) * part, b * width:(b + 1) * width
                ]
        for c in range(cuts):
            send_out(i, c).start()

    mine = pl.ds(pl.multiple_of(chip * chip_rows, chip_rows), chip_rows)

    @pl.loop(0, CHUNKS)
    def _(i):
        total = acc[i, mine, :]
        bulk(a2a.at[i, pl.ds(1, chips - 1)], a2a_send, a2a_recv.at[i], (dp, sibling)).wait_recv()
        for r in range(1, chips):
            total = total + a2a[i, r].astype(F32)
        low, high = total[:rows], total[rows:]
        at = pl.multiple_of(i * chunk, chunk)
        fin_out[:, pl.ds(at, chunk)] = jnp.where(core == 0, high, low)
        in_ref[:, pl.ds(pl.multiple_of(core * half + at, chunk), chunk)] = jnp.where(core == 0, low, high)

    fin = pltpu.make_async_remote_copy(
        src_ref=fin_out, dst_ref=fin_in, send_sem=fin_send, recv_sem=fin_recv,
        device_id=(dp, sibling), device_id_type=MESH,
    )
    fin.start()

    bulk(sib_out, half_send, half_recv.at[0], (dp, sibling)).wait_send()
    bulk(chip_sum.at[:, pl.ds(1, chips - 1)], a2a_send, a2a_recv.at[0], (dp, sibling)).wait_send()
    bulk(tok, sib_send, sib_recv.at[0, 0], (dp, sibling)).wait_send()
    bulk(tok.at[0, pl.ds(0, 2 * (chips - 2))], x_send, x_recv.at[0], (1 - dp, col)).wait_send()
    bulk(tok.at[:, pl.ds(0, chips + 1)], ring_send, ring_recv.at[0, 0, 0], (dp, right)).wait_send()
    zero_out.wait()
    all_out = pl.ds(0, zero_at)
    pltpu.make_async_copy(blocks.at[all_out], out_ref.at[all_out], out_sem).wait()

    fin.wait()
    in_ref[:, pl.ds(pl.multiple_of((1 - core) * half, half), half)] = fin_in[...]


def gather_kernel(
    count_ref, target_ref, block_ref, sum_ref, blocks_ref, in_ref, wg_ref, buf, in_sem, out_sem
):
    n_slots = wg_ref.shape[0]
    chunks = in_sem.shape[0]
    per_chunk = n_slots // chunks
    zero_at = blocks_ref.shape[0] - 1
    targets = 3 * (n_slots // SPC)
    per_piece = targets * GROUP
    count = count_ref[0]

    @pl.loop(0, chunks)
    def _(c):
        for j in range(per_chunk):
            s = c * per_chunk + j
            f = block_ref[s]
            at = (f // GROUP) * per_piece + target_ref[s] * GROUP + f % GROUP
            pltpu.make_async_copy(
                blocks_ref.at[jnp.where(s < count, at, zero_at)], buf.at[s], in_sem.at[c]
            ).start()

    in_ref[...] = sum_ref[...].astype(BF16)

    def out(c):
        at = pl.ds(c * per_chunk, per_chunk)
        return pltpu.make_async_copy(buf.at[at], wg_ref.at[at], out_sem.at[c])

    @pl.loop(0, chunks)
    def _(c):
        at = pl.ds(c * per_chunk, per_chunk)
        pltpu.make_async_copy(blocks_ref.at[pl.ds(0, per_chunk)], buf.at[at], in_sem.at[c]).wait()
        out(c).start()

    @pl.loop(0, chunks)
    def _(c):
        out(c).wait()


def kernel_shards(n_cols, tokens, cotangent, block_weights, slot_block, slot_target, counts):
    n_slots, width = block_weights.shape[:2]
    n_dp = 2
    part = width // n_dp
    rows, features = tokens.shape
    n_f = features // width
    hidden_blocks = n_slots // SPC
    hidden = hidden_blocks * width
    places = 3 * hidden_blocks * n_f
    chips = n_cols // 2
    group_rows = rows * n_cols
    half = features // 2
    dma = pltpu.SemaphoreType.DMA
    vmem = pl.BlockSpec(memory_space=pltpu.VMEM)
    smem = pl.BlockSpec(memory_space=pltpu.SMEM)
    hbm = pl.BlockSpec(memory_space=pl.ANY)
    table_shape = (places // LANES, LANES)
    slot_rows = (n_slots // LANES, LANES)
    input_sum, grad_blocks = pl.pallas_call(
        functools.partial(layer_kernel, n_cols),
        out_shape=(
            jax.ShapeDtypeStruct((rows, features), F32),
            jax.ShapeDtypeStruct((places + 1, part, width), BF16),
        ),
        in_specs=[smem, vmem, vmem, hbm, hbm, hbm],
        out_specs=(vmem, hbm),
        scratch_shapes=[
            pltpu.VMEM((n_dp, n_cols, rows, features), BF16),
            pltpu.VMEM((n_dp, n_cols, rows, features), BF16),
            pltpu.VMEM((places + 1, part, width), BF16),
            pltpu.VMEM((features, 2 * hidden), BF16),
            pltpu.VMEM((hidden, features), BF16),
            pltpu.VMEM((n_dp, group_rows, 2 * hidden), BF16),
            pltpu.VMEM((n_dp, group_rows, hidden), BF16),
            pltpu.VMEM((chips // 2, 2, group_rows, hidden // (chips // 2)), F32),
            pltpu.VMEM((CHUNKS, group_rows, half // CHUNKS), F32),
            pltpu.VMEM((CHUNKS, group_rows, half // CHUNKS), BF16),
            pltpu.VMEM((CHUNKS, group_rows, half // CHUNKS), BF16),
            pltpu.VMEM((CHUNKS, chips, group_rows // chips, half // CHUNKS), BF16),
            pltpu.VMEM((CHUNKS, chips, group_rows // chips, half // CHUNKS), BF16),
            pltpu.VMEM((rows, half), F32),
            pltpu.VMEM((rows, half), F32),
            pltpu.VMEM((4 * part, n_dp * group_rows), BF16),
            pltpu.VMEM((hidden // n_dp, n_dp * group_rows), BF16),
            pltpu.VMEM(table_shape, jnp.int32),
            pltpu.SMEM(table_shape, jnp.int32),
            dma, dma((2,)), dma, dma,
            dma, dma((chips // 2 + 1, 2, 4)),
            dma, dma((2, 2)),
            dma, dma((chips,)), dma, dma((CHUNKS,)),
            dma, dma((CHUNKS,)), dma, dma,
        ],
        compiler_params=pltpu.CompilerParams(
            collective_id=0, has_side_effects=True, vmem_limit_bytes=67043328
        ),
    )(
        counts, slot_target.reshape(slot_rows), slot_block.reshape(slot_rows), tokens, cotangent,
        block_weights.reshape(n_slots * n_dp, part, width),
    )
    gathers = 8
    return pl.pallas_call(
        gather_kernel,
        out_shape=(
            jax.ShapeDtypeStruct((rows, features), BF16),
            jax.ShapeDtypeStruct((n_slots, part, width), BF16),
        ),
        in_specs=[smem, smem, smem, vmem, hbm],
        out_specs=(vmem, hbm),
        scratch_shapes=[
            pltpu.VMEM((n_slots, part, width), BF16), dma((gathers,)), dma((gathers,)),
        ],
    )(counts, slot_target, slot_block, input_sum, grad_blocks)


def solution(mesh):
    n_dp, n_cols = mesh.shape["dp"], mesh.shape["cols"]
    paired = n_dp == 2 and n_cols % 4 == 0

    def body(*args):
        tokens, weights = args[0], args[2]
        if paired and tokens.shape[0] % 16 == 0 and weights.shape[0] % LANES == 0 and weights.shape[0] // SPC % (n_cols // 4) == 0:
            return kernel_shards(n_cols, *args)
        return shards(*args)

    return jax.shard_map(
        body,
        mesh=mesh,
        in_specs=(
            P(("dp", "cols"), None),
            P(("dp", "cols"), None),
            P("cols", None, None),
            P("cols"),
            P("cols"),
            P("cols"),
        ),
        out_specs=(P(("dp", "cols"), None), P("cols", "dp", None)),
        check_vma=False,
    )
```

```python
import functools

import jax
import jax.numpy as jnp
from jax import lax
from jax.experimental import pallas as pl
from jax.experimental.pallas import tpu as pltpu
from jax.sharding import PartitionSpec as P

SPC = 32


def block_inputs(grad_rows, weights, block_select):
    partial_rows = jnp.einsum(
        "rsj,skj->rsk", grad_rows, weights, preferred_element_type=jnp.float32
    )
    summed = jnp.einsum("rsk,sb->rbk", partial_rows, block_select)
    return summed.reshape(summed.shape[0], summed.shape[1] * summed.shape[2])


def shards(tokens, cotangent, block_weights, slot_block, slot_target, counts):
    slot_total = block_weights.shape[0]
    block_width = block_weights.shape[1]
    columns = slot_total // SPC
    features = tokens.shape[1]
    block_count = features // block_width
    tokens_all, cot_all = (
        lax.all_gather(tokens, "cols", axis=0, tiled=True),
        lax.all_gather(cotangent, "cols", axis=0, tiled=True),
    )
    row_total = tokens_all.shape[0]
    live_slot = jnp.arange(slot_total) < counts[0]
    slot_kind = slot_target // columns
    places = slot_target % columns
    up_mask = (live_slot & (slot_kind < 2))[:, None].astype(jnp.float32)
    down_mask = (live_slot & (slot_kind == 2))[:, None].astype(jnp.float32)
    select_up = jax.nn.one_hot(slot_target, 2 * columns, dtype=jnp.float32) * up_mask
    select_down = jax.nn.one_hot(places, columns, dtype=jnp.float32) * down_mask
    block_select = jax.nn.one_hot(slot_block, block_count, dtype=jnp.float32)
    tokens_slots = jnp.take(
        tokens_all.reshape(row_total, block_count, block_width), slot_block, axis=1
    )
    products = jnp.einsum(
        "rsk,skj->rsj", tokens_slots, block_weights, preferred_element_type=jnp.float32
    )
    gate_up = jnp.einsum("rsj,sc->rcj", products, select_up)
    gate_pre = gate_up[:, :columns]
    up_pre = gate_up[:, columns:]
    sigmoid_gate = jax.nn.sigmoid(gate_pre)
    silu_gate = gate_pre * sigmoid_gate
    hidden = (silu_gate * up_pre).astype(jnp.bfloat16)
    cot_slots = jnp.take(cot_all.reshape(row_total, block_count, block_width), slot_block, axis=1)
    back_products = jnp.einsum(
        "rsj,skj->rsk", cot_slots, block_weights, preferred_element_type=jnp.float32
    )
    hidden_grad = jnp.einsum("rsk,sc->rck", back_products, select_down)
    gate_grad = (
        hidden_grad * up_pre * sigmoid_gate * (1.0 + gate_pre * (1.0 - sigmoid_gate))
    ).astype(jnp.bfloat16)
    up_grad = (hidden_grad * silu_gate).astype(jnp.bfloat16)
    pre_grad = jnp.concatenate([gate_grad, up_grad], axis=1)
    slot_grad = jnp.einsum(
        "rck,sc->rsk", pre_grad, select_up.astype(jnp.bfloat16), preferred_element_type=jnp.float32
    ).astype(jnp.bfloat16)
    slot_hidden = jnp.einsum(
        "rck,sc->rsk", hidden, select_down.astype(jnp.bfloat16), preferred_element_type=jnp.float32
    ).astype(jnp.bfloat16)
    weight_terms = jnp.einsum(
        "rsk,rsj->skj", tokens_slots, slot_grad, preferred_element_type=jnp.float32
    )
    weight_terms = weight_terms + jnp.einsum(
        "rsk,rsj->skj", slot_hidden, cot_slots, preferred_element_type=jnp.float32
    )
    input_terms = block_inputs(slot_grad, block_weights, block_select)
    input_sum = lax.psum_scatter(input_terms, "cols", scatter_dimension=0, tiled=True)
    input_grad = input_sum.astype(jnp.bfloat16)
    weight_sum = lax.psum_scatter(
        weight_terms.astype(jnp.bfloat16), "dp", scatter_dimension=1, tiled=True
    )
    return (input_grad, weight_sum)


MESH = pl.DeviceIdType.MESH
F32 = jnp.float32
BF16 = jnp.bfloat16
NT = (((1,), (1,)), ((), ()))
CHUNKS = 4
GROUP = 4
VMEM_LIMIT = 58720256
LANES = 128


def layer_kernel(
    n_cols, count_ref, target_ref, block_ref, tok_ref, cot_ref, w_ref, in_ref, out_ref,
    tok, cot, blocks, wgu, wd, grads, hid, acc, sib_out, sib_in, chip_sum, a2a,
    fin_out, fin_in, lhs, hid_t, table_rows, table_ref,
    w_sem, own_sem, table_sem, ring_send, ring_recv, sib_send, sib_recv,
    x_send, x_recv, half_send, half_recv, a2a_send, a2a_recv, fin_send, fin_recv,
):
    chips = n_cols // 2
    steps = chips // 2
    rows = tok_ref.shape[0]
    group_rows = rows * n_cols
    features = tok_ref.shape[1]
    width = blocks.shape[2]
    part = blocks.shape[1]
    n_f = features // width
    hidden = wd.shape[0]
    n_h = hidden // width
    zero_at = blocks.shape[0] - 1
    zero_slot = zero_at
    table_size = zero_slot // LANES
    n_slots = out_ref.shape[0]
    half = features // 2
    dp = lax.axis_index("dp")
    col = lax.axis_index("cols")
    core = col % 2
    chip = col // 2
    place = jnp.where(chip % 2 == 0, chip // 2, chips - 1 - chip // 2)

    def chip_at(p):
        p = (p + 2 * chips) % chips
        return jnp.where(p < steps, 2 * p, 2 * (chips - 1 - p) + 1)

    right = chip_at(place + 1) * 2 + core
    left = chip_at(place - 1) * 2 + core
    sibling = chip * 2 + 1 - core
    sides = ((tok_ref, tok), (cot_ref, cot))

    owns = [pltpu.make_async_copy(sides[a][0], sides[a][1].at[0, col], own_sem.at[a]) for a in range(2)]
    for own in owns:
        own.start()
    w_copy = pltpu.make_async_copy(w_ref, blocks.at[pl.ds(0, w_ref.shape[0])], w_sem)
    w_copy.start()
    barrier = pltpu.get_barrier_semaphore()
    for r in range(1, chips):
        pl.semaphore_signal(barrier, inc=1, device_id=(dp, ((chip + r) % chips) * 2 + core), device_id_type=MESH)
    pl.semaphore_signal(barrier, inc=1, device_id=(dp, sibling), device_id_type=MESH)
    pl.semaphore_signal(barrier, inc=1, device_id=(1 - dp, col), device_id_type=MESH)
    pl.semaphore_wait(barrier, chips + 1)

    def piece(g, origin, a):
        at = pl.ds((a % 2) * half, half)
        return sides[a // 2][1].at[g, origin * 2 + core, :, at]

    def ring_copy(g, origin, direction, s, a):
        block = piece(g, origin, a)
        return pltpu.make_async_remote_copy(
            src_ref=block, dst_ref=block,
            send_sem=ring_send, recv_sem=ring_recv.at[g * steps + s, direction, a],
            device_id=(dp, right if direction == 0 else left), device_id_type=MESH,
        )

    def ring(g, direction, s, a):
        return ring_copy(g, chip_at(place - s if direction == 0 else place + s), direction, s, a)

    def ring_arrival(g, direction, s, a):
        return ring_copy(g, chip_at(place - 1 - s if direction == 0 else place + 1 + s), direction, s, a)

    def share_copy(g, k, a, lane):
        at = pl.ds((a % 2) * half, half)
        block = sides[a // 2][1].at[g, chip_at(place - k) * 2 + lane, :, at]
        return pltpu.make_async_remote_copy(
            src_ref=block, dst_ref=block,
            send_sem=sib_send, recv_sem=sib_recv.at[g, a // 2],
            device_id=(dp, sibling), device_id_type=MESH,
        )

    def share(g, k, a):
        return share_copy(g, k, a, core)

    def cross(k, a):
        origin = chip_at(place - k)
        return pltpu.make_async_remote_copy(
            src_ref=piece(0, origin, a), dst_ref=piece(1, origin, a),
            send_sem=x_send, recv_sem=x_recv.at[k],
            device_id=(1 - dp, col), device_id_type=MESH,
        )

    def first(g, arr):
        for a in (2 * arr, 2 * arr + 1):
            for direction in range(2):
                ring(g, direction, 0, a).start()
        for a in (2 * arr, 2 * arr + 1):
            share(g, 0, a).start()
            if g == 0:
                cross(0, a).start()

    def pass_on(s, direction, a):
        ring_arrival(0, direction, s, a).wait_recv()

        far = steps - 1 if a % 2 == direction else steps - 2

        @pl.when(s < far)
        def _():
            ring(0, direction, s + 1, a).start()

        k = 1 + s if direction == 0 else chips - 1 - s
        share(0, k, a).start()

        @pl.when(s > 0)
        def _():
            cross(k, a).start()

    def advance(s, arr):
        for direction in range(2):
            pass_on(s, direction, 2 * arr + direction)

        @pl.when(s < steps - 1)
        def _():
            for direction in range(2):
                pass_on(s, direction, 2 * arr + 1 - direction)

    def bulk(ref, send_sem, recv_sem, device):
        return pltpu.make_async_remote_copy(
            src_ref=ref, dst_ref=ref, send_sem=send_sem, recv_sem=recv_sem,
            device_id=device, device_id_type=MESH,
        )

    def all_shared(g, arr):
        bulk(sides[arr][1].at[g, pl.ds(0, chips)], sib_send, sib_recv.at[g, arr], (dp, sibling)).wait_recv()

    def cross_arrival(k):
        bulk(tok.at[1, pl.ds(0, 2)], x_send, x_recv.at[k], (1 - dp, col)).wait_recv()

    def crossed(k):
        cross_arrival(k)
        for a in range(4):
            share(1, k, a).start()

    for own in owns:
        own.wait()
    first(0, 0)

    slot_place = target_ref[...] * n_f + block_ref[...]
    number = lax.broadcasted_iota(jnp.int32, slot_place.shape, 0) * LANES + lax.broadcasted_iota(
        jnp.int32, slot_place.shape, 1
    )
    live = number < count_ref[0]
    slot_place = jnp.where(live, slot_place, -1)
    table_rows[table_size:, :] = jnp.where(live, slot_place, zero_at)
    lane = lax.broadcasted_iota(jnp.int32, (LANES, LANES), 1)
    in_row = lax.broadcasted_iota(jnp.int32, (LANES, LANES), 0)
    columns = [
        jnp.broadcast_to(slot_place[j:j + 1], (LANES, LANES)).T for j in range(slot_place.shape[0])
    ]
    for t in range(zero_slot // LANES):
        row = jnp.zeros((1, LANES), jnp.int32)
        for j, column in enumerate(columns):
            hit = column == lane + t * LANES
            row = row + jnp.sum(
                jnp.where(hit, in_row + (j * LANES - zero_slot), 0), axis=0, keepdims=True
            )
        table_rows[t:t + 1, :] = row + zero_slot
    table_copy = pltpu.make_async_copy(table_rows, table_ref, table_sem)
    table_copy.start()
    blocks[zero_at] = jnp.zeros((part, width), BF16)
    w_copy.wait()
    table_copy.wait()

    pieces = width // part

    def spread(h, f):
        at = pl.multiple_of(f * width, width)
        hid_at = pl.multiple_of(h * width, width)
        for k in range(3):
            entry = (k * n_h + h) * n_f + f
            index = table_ref[entry // LANES, entry % LANES]
            for piece in range(pieces):
                value = blocks[jnp.minimum(index * pieces + piece, zero_at)]
                if k < 2:
                    wgu[pl.ds(pl.multiple_of(at + piece * part, part), part),
                        pl.ds(pl.multiple_of(k * hidden + hid_at, width), width)] = value
                else:
                    wd[pl.ds(pl.multiple_of(hid_at + piece * part, part), part), pl.ds(at, width)] = value

    per_step = n_h // steps

    @pl.loop(0, steps)
    def _(s):
        @pl.loop(0, n_f)
        def _(f):
            for j in range(per_step):
                spread(s * per_step + j, f)

        advance(s, 0)

        @pl.when(s == steps // 2 - 1)
        def _():
            first(0, 1)

    all_shared(0, 0)
    span = hidden // steps

    def before(g, n):
        at = pl.multiple_of(n * span, span)
        x = tok[g].reshape(group_rows, features)
        gate = jnp.dot(x, wgu[:, pl.ds(at, span)], preferred_element_type=F32)
        up = jnp.dot(x, wgu[:, pl.ds(pl.multiple_of(hidden + at, span), span)], preferred_element_type=F32)
        return gate, up

    def after(g, n, gate, up):
        at = pl.multiple_of(n * span, span)
        back = lax.dot_general(
            cot[g].reshape(group_rows, features), wd[pl.ds(at, span), :], NT, preferred_element_type=F32
        )
        sig = jax.nn.sigmoid(gate)
        silu = gate * sig
        hid[g, :, pl.ds(at, span)] = (silu * up).astype(BF16)
        grads[g, :, pl.ds(at, span)] = (back * up * sig * (1.0 + gate * (1.0 - sig))).astype(BF16)
        grads[g, :, pl.ds(pl.multiple_of(hidden + at, span), span)] = (back * silu).astype(BF16)

    @pl.loop(0, steps)
    def _(s):
        gate, up = before(0, s)
        acc[s, :, :span] = gate
        acc[s, :, span:] = up
        advance(s, 1)

    cross_arrival(0)
    first(1, 0)
    first(1, 1)
    all_shared(0, 1)

    @pl.loop(0, steps)
    def _(s):
        after(0, s, acc[s, :, :span], acc[s, :, span:])

    crossed(2)
    crossed(chips - 2)

    chunk = half // CHUNKS
    chip_rows = group_rows // chips

    def terms(at):
        return lax.dot_general(grads[0], wgu[pl.ds(at, chunk), :], NT, preferred_element_type=F32)

    def to_sibling(i):
        return pltpu.make_async_remote_copy(
            src_ref=sib_out.at[i], dst_ref=sib_in.at[i], send_sem=half_send, recv_sem=half_recv.at[i],
            device_id=(dp, sibling), device_id_type=MESH,
        )

    def spread_sum(r, i):
        other = (chip + r) % chips
        return pltpu.make_async_remote_copy(
            src_ref=chip_sum.at[i, other], dst_ref=a2a.at[i, r],
            send_sem=a2a_send, recv_sem=a2a_recv.at[i],
            device_id=(dp, other * 2 + core), device_id_type=MESH,
        )

    def pair_sum(i):
        to_sibling(i).wait_recv()

        @pl.loop(0, chips)
        def _(c):
            at = pl.ds(pl.multiple_of(c * chip_rows, chip_rows), chip_rows)
            total = acc[i, at, :] + sib_in[i, at, :].astype(F32)
            acc[i, at, :] = total
            chip_sum[i, c] = total.astype(BF16)

        @pl.loop(1, chips)
        def _(r):
            spread_sum(r, i).start()

    @pl.loop(0, CHUNKS)
    def _(i):
        at = pl.multiple_of(i * chunk, chunk)
        sib_out[i] = terms(pl.multiple_of((1 - core) * half + at, chunk)).astype(BF16)
        to_sibling(i).start()
        acc[i] = terms(pl.multiple_of(core * half + at, chunk))

        @pl.when(i > 0)
        def _():
            pair_sum(i - 1)

    pair_sum(CHUNKS - 1)

    for direction in range(2):
        for a in range(4):
            ring_arrival(1, direction, 0, a).wait_recv()
            share(1, 1 if direction == 0 else chips - 1, a).start()

    @pl.loop(3, chips - 2)
    def _(k):
        crossed(k)

    all_shared(1, 0)
    all_shared(1, 1)

    @pl.loop(0, steps)
    def _(s):
        gate, up = before(1, s)
        after(1, s, gate, up)

    def take_part(block):
        out = block[:part]
        for i in range(1, width // part):
            out = jnp.where(dp == i, block[i * part:(i + 1) * part], out)
        return out

    for g in range(2):
        for h in range(n_h):
            hid_t[pl.ds(h * part, part), pl.ds(g * group_rows, group_rows)] = take_part(
                hid[g, :, pl.ds(h * width, width)].T
            )
    four = GROUP
    @pl.loop(0, n_f // four)
    def _(i):
        at = pl.multiple_of(i * four * width, four * width)
        for g in range(2):
            for b in range(four):
                piece = tok[g, :, :, pl.ds(pl.multiple_of(at + b * width, width), width)]
                lhs[pl.ds(b * part, part), pl.ds(g * group_rows, group_rows)] = take_part(
                    piece.reshape(group_rows, width).T
                )
        for n in range(2 * n_h // 4):
            cut = slice(n * 4 * width, (n + 1) * 4 * width)
            out = jnp.dot(
                lhs[...], grads[:, :, cut].reshape(2 * group_rows, 4 * width), preferred_element_type=F32
            ).astype(BF16)
            for h in range(4):
                for b in range(four):
                    blocks[(n * 4 + h) * n_f + i * four + b] = out[
                        b * part:(b + 1) * part, h * width:(h + 1) * width
                    ]
        c = cot[:, :, :, pl.ds(at, four * width)].reshape(2 * group_rows, four * width)
        out = jnp.dot(hid_t[...], c, preferred_element_type=F32).astype(BF16)
        for h in range(n_h):
            for b in range(four):
                blocks[(2 * n_h + h) * n_f + i * four + b] = out[
                    h * part:(h + 1) * part, b * width:(b + 1) * width
                ]

    for r in range(n_slots // LANES):
        @pl.loop(0, LANES, unroll=8)
        def _(j):
            out_ref[r * LANES + j] = blocks[table_ref[table_size + r, j]]

    mine = pl.ds(pl.multiple_of(chip * chip_rows, chip_rows), chip_rows)

    @pl.loop(0, CHUNKS)
    def _(i):
        total = acc[i, mine, :]
        bulk(a2a.at[i, pl.ds(1, chips - 1)], a2a_send, a2a_recv.at[i], (dp, sibling)).wait_recv()
        for r in range(1, chips):
            total = total + a2a[i, r].astype(F32)
        low, high = total[:rows], total[rows:]
        at = pl.multiple_of(i * chunk, chunk)
        fin_out[:, pl.ds(at, chunk)] = jnp.where(core == 0, high, low)
        in_ref[:, pl.ds(pl.multiple_of(core * half + at, chunk), chunk)] = jnp.where(
            core == 0, low, high
        ).astype(BF16)

    fin = pltpu.make_async_remote_copy(
        src_ref=fin_out, dst_ref=fin_in, send_sem=fin_send, recv_sem=fin_recv,
        device_id=(dp, sibling), device_id_type=MESH,
    )
    fin.start()

    bulk(sib_out, half_send, half_recv.at[0], (dp, sibling)).wait_send()
    bulk(chip_sum.at[:, pl.ds(1, chips - 1)], a2a_send, a2a_recv.at[0], (dp, sibling)).wait_send()
    bulk(tok, sib_send, sib_recv.at[0, 0], (dp, sibling)).wait_send()
    bulk(tok.at[0, pl.ds(0, 2 * (chips - 2))], x_send, x_recv.at[0], (1 - dp, col)).wait_send()
    bulk(tok.at[:, pl.ds(0, chips + 1)], ring_send, ring_recv.at[0, 0, 0], (dp, right)).wait_send()
    fin.wait()
    in_ref[:, pl.ds(pl.multiple_of((1 - core) * half, half), half)] = fin_in[...].astype(BF16)


def kernel_shards(n_cols, tokens, cotangent, block_weights, slot_block, slot_target, counts):
    n_slots, width = block_weights.shape[:2]
    n_dp = 2
    part = width // n_dp
    rows, features = tokens.shape
    n_f = features // width
    hidden_blocks = n_slots // SPC
    hidden = hidden_blocks * width
    places = 3 * hidden_blocks * n_f
    chips = n_cols // 2
    group_rows = rows * n_cols
    half = features // 2
    dma = pltpu.SemaphoreType.DMA
    vmem = pl.BlockSpec(memory_space=pltpu.VMEM)
    smem = pl.BlockSpec(memory_space=pltpu.SMEM)
    hbm = pl.BlockSpec(memory_space=pl.ANY)
    table_shape = (places // LANES + n_slots // LANES, LANES)
    slot_rows = (n_slots // LANES, LANES)
    return pl.pallas_call(
        functools.partial(layer_kernel, n_cols),
        out_shape=(
            pltpu.VMEM((rows, features), BF16),
            pltpu.VMEM((n_slots, part, width), BF16),
        ),
        in_specs=[smem, vmem, vmem, hbm, hbm, hbm],
        out_specs=(vmem, vmem),
        scratch_shapes=[
            pltpu.VMEM((n_dp, n_cols, rows, features), BF16),
            pltpu.VMEM((n_dp, n_cols, rows, features), BF16),
            pltpu.VMEM((places + 1, part, width), BF16),
            pltpu.VMEM((features, 2 * hidden), BF16),
            pltpu.VMEM((hidden, features), BF16),
            pltpu.VMEM((n_dp, group_rows, 2 * hidden), BF16),
            pltpu.VMEM((n_dp, group_rows, hidden), BF16),
            pltpu.VMEM((CHUNKS, group_rows, half // CHUNKS), F32),
            pltpu.VMEM((CHUNKS, group_rows, half // CHUNKS), BF16),
            pltpu.VMEM((CHUNKS, group_rows, half // CHUNKS), BF16),
            pltpu.VMEM((CHUNKS, chips, group_rows // chips, half // CHUNKS), BF16),
            pltpu.VMEM((CHUNKS, chips, group_rows // chips, half // CHUNKS), BF16),
            pltpu.VMEM((rows, half), F32),
            pltpu.VMEM((rows, half), F32),
            pltpu.VMEM((4 * part, n_dp * group_rows), BF16),
            pltpu.VMEM((hidden // n_dp, n_dp * group_rows), BF16),
            pltpu.VMEM(table_shape, jnp.int32),
            pltpu.SMEM(table_shape, jnp.int32),
            dma, dma((2,)), dma,
            dma, dma((chips // 2 + 1, 2, 4)),
            dma, dma((2, 2)),
            dma, dma((chips,)), dma, dma((CHUNKS,)),
            dma, dma((CHUNKS,)), dma, dma,
        ],
        compiler_params=pltpu.CompilerParams(
            collective_id=0, has_side_effects=True, vmem_limit_bytes=VMEM_LIMIT
        ),
    )(
        counts, slot_target.reshape(slot_rows), slot_block.reshape(slot_rows), tokens, cotangent,
        block_weights.reshape(n_slots * n_dp, part, width),
    )


def solution(mesh):
    n_dp, n_cols = mesh.shape["dp"], mesh.shape["cols"]
    paired = n_dp == 2 and n_cols % 4 == 0

    def body(*args):
        tokens, weights = args[0], args[2]
        if paired and tokens.shape[0] % 16 == 0 and weights.shape[0] % LANES == 0 and weights.shape[0] // SPC % (n_cols // 4) == 0:
            return kernel_shards(n_cols, *args)
        return shards(*args)

    return jax.shard_map(
        body,
        mesh=mesh,
        in_specs=(
            P(("dp", "cols"), None),
            P(("dp", "cols"), None),
            P("cols", None, None),
            P("cols"),
            P("cols"),
            P("cols"),
        ),
        out_specs=(P(("dp", "cols"), None), P("cols", "dp", None)),
        check_vma=False,
    )
```

```python
import functools

import jax
import jax.numpy as jnp
from jax import lax
from jax.experimental import pallas as pl
from jax.experimental.pallas import tpu as pltpu
from jax.sharding import PartitionSpec as P

SPC = 32


def block_inputs(grad_rows, weights, block_select):
    partial_rows = jnp.einsum(
        "rsj,skj->rsk", grad_rows, weights, preferred_element_type=jnp.float32
    )
    summed = jnp.einsum("rsk,sb->rbk", partial_rows, block_select)
    return summed.reshape(summed.shape[0], summed.shape[1] * summed.shape[2])


def shards(tokens, cotangent, block_weights, slot_block, slot_target, counts):
    slot_total = block_weights.shape[0]
    block_width = block_weights.shape[1]
    columns = slot_total // SPC
    features = tokens.shape[1]
    block_count = features // block_width
    tokens_all, cot_all = (
        lax.all_gather(tokens, "cols", axis=0, tiled=True),
        lax.all_gather(cotangent, "cols", axis=0, tiled=True),
    )
    row_total = tokens_all.shape[0]
    live_slot = jnp.arange(slot_total) < counts[0]
    slot_kind = slot_target // columns
    places = slot_target % columns
    up_mask = (live_slot & (slot_kind < 2))[:, None].astype(jnp.float32)
    down_mask = (live_slot & (slot_kind == 2))[:, None].astype(jnp.float32)
    select_up = jax.nn.one_hot(slot_target, 2 * columns, dtype=jnp.float32) * up_mask
    select_down = jax.nn.one_hot(places, columns, dtype=jnp.float32) * down_mask
    block_select = jax.nn.one_hot(slot_block, block_count, dtype=jnp.float32)
    tokens_slots = jnp.take(
        tokens_all.reshape(row_total, block_count, block_width), slot_block, axis=1
    )
    products = jnp.einsum(
        "rsk,skj->rsj", tokens_slots, block_weights, preferred_element_type=jnp.float32
    )
    gate_up = jnp.einsum("rsj,sc->rcj", products, select_up)
    gate_pre = gate_up[:, :columns]
    up_pre = gate_up[:, columns:]
    sigmoid_gate = jax.nn.sigmoid(gate_pre)
    silu_gate = gate_pre * sigmoid_gate
    hidden = (silu_gate * up_pre).astype(jnp.bfloat16)
    cot_slots = jnp.take(cot_all.reshape(row_total, block_count, block_width), slot_block, axis=1)
    back_products = jnp.einsum(
        "rsj,skj->rsk", cot_slots, block_weights, preferred_element_type=jnp.float32
    )
    hidden_grad = jnp.einsum("rsk,sc->rck", back_products, select_down)
    gate_grad = (
        hidden_grad * up_pre * sigmoid_gate * (1.0 + gate_pre * (1.0 - sigmoid_gate))
    ).astype(jnp.bfloat16)
    up_grad = (hidden_grad * silu_gate).astype(jnp.bfloat16)
    pre_grad = jnp.concatenate([gate_grad, up_grad], axis=1)
    slot_grad = jnp.einsum(
        "rck,sc->rsk", pre_grad, select_up.astype(jnp.bfloat16), preferred_element_type=jnp.float32
    ).astype(jnp.bfloat16)
    slot_hidden = jnp.einsum(
        "rck,sc->rsk", hidden, select_down.astype(jnp.bfloat16), preferred_element_type=jnp.float32
    ).astype(jnp.bfloat16)
    weight_terms = jnp.einsum(
        "rsk,rsj->skj", tokens_slots, slot_grad, preferred_element_type=jnp.float32
    )
    weight_terms = weight_terms + jnp.einsum(
        "rsk,rsj->skj", slot_hidden, cot_slots, preferred_element_type=jnp.float32
    )
    input_terms = block_inputs(slot_grad, block_weights, block_select)
    input_sum = lax.psum_scatter(input_terms, "cols", scatter_dimension=0, tiled=True)
    input_grad = input_sum.astype(jnp.bfloat16)
    weight_sum = lax.psum_scatter(
        weight_terms.astype(jnp.bfloat16), "dp", scatter_dimension=1, tiled=True
    )
    return (input_grad, weight_sum)


MESH = pl.DeviceIdType.MESH
F32 = jnp.float32
BF16 = jnp.bfloat16
NT = (((1,), (1,)), ((), ()))
CHUNKS = 4
GROUP = 4
VMEM_LIMIT = 58720256
LANES = 128


def layer_kernel(
    n_cols, count_ref, target_ref, block_ref, tok_ref, cot_ref, w_ref, in_ref, out_ref,
    tok, cot, blocks, wgu, wd, grads, hid, acc, sib_out, sib_in, chip_sum, a2a,
    fin_out, fin_in, lhs, hid_t, table_rows, table_ref,
    w_sem, own_sem, table_sem, ring_send, ring_recv, sib_send, sib_recv,
    x_send, x_recv, half_send, half_recv, a2a_send, a2a_recv, fin_send, fin_recv,
):
    chips = n_cols // 2
    steps = chips // 2
    rows = tok_ref.shape[0]
    group_rows = rows * n_cols
    features = tok_ref.shape[1]
    width = blocks.shape[2]
    part = blocks.shape[1]
    n_f = features // width
    hidden = wd.shape[0]
    n_h = hidden // width
    zero_at = blocks.shape[0] - 1
    zero_slot = zero_at
    table_size = zero_slot // LANES
    n_slots = out_ref.shape[0]
    half = features // 2
    dp = lax.axis_index("dp")
    col = lax.axis_index("cols")
    core = col % 2
    chip = col // 2
    place = jnp.where(chip % 2 == 0, chip // 2, chips - 1 - chip // 2)

    def chip_at(p):
        p = (p + 2 * chips) % chips
        return jnp.where(p < steps, 2 * p, 2 * (chips - 1 - p) + 1)

    right = chip_at(place + 1) * 2 + core
    left = chip_at(place - 1) * 2 + core
    sibling = chip * 2 + 1 - core
    sides = ((tok_ref, tok), (cot_ref, cot))

    owns = [pltpu.make_async_copy(sides[a][0], sides[a][1].at[0, col], own_sem.at[a]) for a in range(2)]
    for own in owns:
        own.start()
    w_copy = pltpu.make_async_copy(w_ref, blocks.at[pl.ds(0, w_ref.shape[0])], w_sem)
    barrier = pltpu.get_barrier_semaphore()
    for r in range(1, chips):
        pl.semaphore_signal(barrier, inc=1, device_id=(dp, ((chip + r) % chips) * 2 + core), device_id_type=MESH)
    pl.semaphore_signal(barrier, inc=1, device_id=(dp, sibling), device_id_type=MESH)
    pl.semaphore_signal(barrier, inc=1, device_id=(1 - dp, col), device_id_type=MESH)
    pl.semaphore_wait(barrier, chips + 1)

    def piece(g, origin, a):
        at = pl.ds((a % 2) * half, half)
        return sides[a // 2][1].at[g, origin * 2 + core, :, at]

    def ring_copy(g, origin, direction, s, a):
        block = piece(g, origin, a)
        return pltpu.make_async_remote_copy(
            src_ref=block, dst_ref=block,
            send_sem=ring_send, recv_sem=ring_recv.at[g * steps + s, direction, a],
            device_id=(dp, right if direction == 0 else left), device_id_type=MESH,
        )

    def ring(g, direction, s, a):
        return ring_copy(g, chip_at(place - s if direction == 0 else place + s), direction, s, a)

    def ring_arrival(g, direction, s, a):
        return ring_copy(g, chip_at(place - 1 - s if direction == 0 else place + 1 + s), direction, s, a)

    def share_copy(g, k, a, lane):
        at = pl.ds((a % 2) * half, half)
        block = sides[a // 2][1].at[g, chip_at(place - k) * 2 + lane, :, at]
        return pltpu.make_async_remote_copy(
            src_ref=block, dst_ref=block,
            send_sem=sib_send, recv_sem=sib_recv.at[g, a // 2],
            device_id=(dp, sibling), device_id_type=MESH,
        )

    def share(g, k, a):
        return share_copy(g, k, a, core)

    def cross(k, a):
        origin = chip_at(place - k)
        return pltpu.make_async_remote_copy(
            src_ref=piece(0, origin, a), dst_ref=piece(1, origin, a),
            send_sem=x_send, recv_sem=x_recv.at[k],
            device_id=(1 - dp, col), device_id_type=MESH,
        )

    def piece_of(arr, direction, far):
        return 2 * arr + (direction if far else 1 - direction)

    def send(g, arr, s, far):
        for direction in range(2):
            ring(g, direction, s, piece_of(arr, direction, far)).start()

    def arrive(arr, s, far, forward):
        for direction in range(2):
            a = piece_of(arr, direction, far)
            ring_arrival(0, direction, s, a).wait_recv()
            if forward and s < (steps - 1 if far else steps - 2):
                ring(0, direction, s + 1, a).start()
            k = 1 + s if direction == 0 else chips - 1 - s
            share(0, k, a).start()
            if s > 1 or (s == 1 and not far):
                cross(k, a).start()

    def passed(s, far):
        arrive(1, s, far, True)

    def arrive_other(s, far):
        for direction in range(2):
            for arr in range(2):
                a = piece_of(arr, direction, far)
                ring_arrival(1, direction, s, a).wait_recv()
                if far and s == 0:
                    ring(1, direction, 1, a).start()
                share(1, 1 + s if direction == 0 else chips - 1 - s, a).start()

    def bulk(ref, send_sem, recv_sem, device):
        return pltpu.make_async_remote_copy(
            src_ref=ref, dst_ref=ref, send_sem=send_sem, recv_sem=recv_sem,
            device_id=device, device_id_type=MESH,
        )

    def all_shared(g, arr):
        bulk(sides[arr][1].at[g, pl.ds(0, chips)], sib_send, sib_recv.at[g, arr], (dp, sibling)).wait_recv()

    def cross_arrival(k, count=2):
        bulk(tok.at[1, pl.ds(0, count)], x_send, x_recv.at[k], (1 - dp, col)).wait_recv()

    def crossed(k, pieces=range(4)):
        cross_arrival(k, len(pieces) // 2)
        for a in pieces:
            share(1, k, a).start()

    for own in owns:
        own.wait()
    w_copy.start()
    send(0, 0, 0, True)
    send(0, 0, 0, False)
    send(0, 1, 0, True)
    for a in range(4):
        cross(0, a).start()
        share(0, 0, a).start()

    slot_place = target_ref[...] * n_f + block_ref[...]
    number = lax.broadcasted_iota(jnp.int32, slot_place.shape, 0) * LANES + lax.broadcasted_iota(
        jnp.int32, slot_place.shape, 1
    )
    live = number < count_ref[0]
    slot_place = jnp.where(live, slot_place, -1)
    table_rows[table_size:, :] = jnp.where(live, slot_place, zero_at)
    lane = lax.broadcasted_iota(jnp.int32, (LANES, LANES), 1)
    in_row = lax.broadcasted_iota(jnp.int32, (LANES, LANES), 0)
    columns = [
        jnp.broadcast_to(slot_place[j:j + 1], (LANES, LANES)).T for j in range(slot_place.shape[0])
    ]
    for t in range(zero_slot // LANES):
        row = jnp.zeros((1, LANES), jnp.int32)
        for j, column in enumerate(columns):
            hit = column == lane + t * LANES
            row = row + jnp.sum(
                jnp.where(hit, in_row + (j * LANES - zero_slot), 0), axis=0, keepdims=True
            )
        table_rows[t:t + 1, :] = row + zero_slot
    table_copy = pltpu.make_async_copy(table_rows, table_ref, table_sem)
    table_copy.start()
    blocks[zero_at] = jnp.zeros((part, width), BF16)
    w_copy.wait()
    table_copy.wait()

    pieces = width // part

    def spread(h, f):
        at = pl.multiple_of(f * width, width)
        hid_at = pl.multiple_of(h * width, width)
        for k in range(3):
            entry = (k * n_h + h) * n_f + f
            index = table_ref[entry // LANES, entry % LANES]
            for piece in range(pieces):
                value = blocks[jnp.minimum(index * pieces + piece, zero_at)]
                if k < 2:
                    wgu[pl.ds(pl.multiple_of(at + piece * part, part), part),
                        pl.ds(pl.multiple_of(k * hidden + hid_at, width), width)] = value
                else:
                    wd[pl.ds(pl.multiple_of(hid_at + piece * part, part), part), pl.ds(at, width)] = value

    per_step = n_h // steps

    waiting = [(s, far) for s in range(steps) for far in (True, False) if far or s < steps - 1]
    for s in range(steps):
        @pl.loop(0, n_f)
        def _(f):
            for j in range(per_step):
                spread(s * per_step + j, f)

        arrive(0, s, True, True)
        if s < steps - 1:
            arrive(0, s, False, True)
        if s == 0:
            send(0, 1, 0, False)
        for _ in range(min(s, 1) + (s == steps - 1)):
            passed(*waiting.pop(0))

    all_shared(0, 0)
    span = hidden // steps

    def before(g, n):
        at = pl.multiple_of(n * span, span)
        x = tok[g].reshape(group_rows, features)
        gate = jnp.dot(x, wgu[:, pl.ds(at, span)], preferred_element_type=F32)
        up = jnp.dot(x, wgu[:, pl.ds(pl.multiple_of(hidden + at, span), span)], preferred_element_type=F32)
        return gate, up

    def after(g, n, gate, up):
        at = pl.multiple_of(n * span, span)
        back = lax.dot_general(
            cot[g].reshape(group_rows, features), wd[pl.ds(at, span), :], NT, preferred_element_type=F32
        )
        sig = jax.nn.sigmoid(gate)
        silu = gate * sig
        hid[g, :, pl.ds(at, span)] = (silu * up).astype(BF16)
        grads[g, :, pl.ds(at, span)] = (back * up * sig * (1.0 + gate * (1.0 - sig))).astype(BF16)
        grads[g, :, pl.ds(pl.multiple_of(hidden + at, span), span)] = (back * silu).astype(BF16)

    for s in range(steps):
        gate, up = before(0, s)
        acc[s, :, :span] = gate
        acc[s, :, span:] = up
        if s < steps - 2:
            passed(*waiting.pop(0))
        if s == steps - 3:
            cross_arrival(0)
            for far in (True, False):
                for arr in range(2):
                    send(1, arr, 0, far)
            for a in range(4):
                share(1, 0, a).start()

    while waiting:
        passed(*waiting.pop(0))

    all_shared(0, 1)

    @pl.loop(0, steps)
    def _(s):
        after(0, s, acc[s, :, :span], acc[s, :, span:])

    crossed(2, (1, 3))
    crossed(chips - 2, (0, 2))
    arrive_other(0, True)

    chunk = half // CHUNKS
    chip_rows = group_rows // chips

    def terms(at):
        return lax.dot_general(grads[0], wgu[pl.ds(at, chunk), :], NT, preferred_element_type=F32)

    def to_sibling(i):
        return pltpu.make_async_remote_copy(
            src_ref=sib_out.at[i], dst_ref=sib_in.at[i], send_sem=half_send, recv_sem=half_recv.at[i],
            device_id=(dp, sibling), device_id_type=MESH,
        )

    def spread_sum(r, i):
        other = (chip + r) % chips
        return pltpu.make_async_remote_copy(
            src_ref=chip_sum.at[i, other], dst_ref=a2a.at[i, r],
            send_sem=a2a_send, recv_sem=a2a_recv.at[i],
            device_id=(dp, other * 2 + core), device_id_type=MESH,
        )

    def pair_sum(i):
        to_sibling(i).wait_recv()

        @pl.loop(0, chips)
        def _(c):
            at = pl.ds(pl.multiple_of(c * chip_rows, chip_rows), chip_rows)
            total = acc[i, at, :] + sib_in[i, at, :].astype(F32)
            acc[i, at, :] = total
            chip_sum[i, c] = total.astype(BF16)

        @pl.loop(1, chips)
        def _(r):
            spread_sum(r, i).start()

    @pl.loop(0, CHUNKS)
    def _(i):
        at = pl.multiple_of(i * chunk, chunk)
        sib_out[i] = terms(pl.multiple_of((1 - core) * half + at, chunk)).astype(BF16)
        to_sibling(i).start()
        acc[i] = terms(pl.multiple_of(core * half + at, chunk))

        @pl.when(i > 0)
        def _():
            pair_sum(i - 1)

        @pl.when(i == 0)
        def _():
            arrive_other(0, False)

        @pl.when(i == CHUNKS - 2)
        def _():
            arrive_other(1, True)
            crossed(3)
            crossed(chips - 3)

    pair_sum(CHUNKS - 1)

    @pl.loop(4, chips - 3)
    def _(k):
        crossed(k)

    all_shared(1, 0)
    all_shared(1, 1)

    @pl.loop(0, steps)
    def _(s):
        gate, up = before(1, s)
        after(1, s, gate, up)

    def take_part(block):
        out = block[:part]
        for i in range(1, width // part):
            out = jnp.where(dp == i, block[i * part:(i + 1) * part], out)
        return out

    for g in range(2):
        for h in range(n_h):
            hid_t[pl.ds(h * part, part), pl.ds(g * group_rows, group_rows)] = take_part(
                hid[g, :, pl.ds(h * width, width)].T
            )
    four = GROUP
    @pl.loop(0, n_f // four)
    def _(i):
        at = pl.multiple_of(i * four * width, four * width)
        for g in range(2):
            for b in range(four):
                piece = tok[g, :, :, pl.ds(pl.multiple_of(at + b * width, width), width)]
                lhs[pl.ds(b * part, part), pl.ds(g * group_rows, group_rows)] = take_part(
                    piece.reshape(group_rows, width).T
                )
        for n in range(2 * n_h // 4):
            cut = slice(n * 4 * width, (n + 1) * 4 * width)
            out = jnp.dot(
                lhs[...], grads[:, :, cut].reshape(2 * group_rows, 4 * width), preferred_element_type=F32
            ).astype(BF16)
            for h in range(4):
                for b in range(four):
                    blocks[(n * 4 + h) * n_f + i * four + b] = out[
                        b * part:(b + 1) * part, h * width:(h + 1) * width
                    ]
        c = cot[:, :, :, pl.ds(at, four * width)].reshape(2 * group_rows, four * width)
        out = jnp.dot(hid_t[...], c, preferred_element_type=F32).astype(BF16)
        for h in range(n_h):
            for b in range(four):
                blocks[(2 * n_h + h) * n_f + i * four + b] = out[
                    h * part:(h + 1) * part, b * width:(b + 1) * width
                ]

    for r in range(n_slots // LANES):
        @pl.loop(0, LANES, unroll=8)
        def _(j):
            out_ref[r * LANES + j] = blocks[table_ref[table_size + r, j]]

    mine = pl.ds(pl.multiple_of(chip * chip_rows, chip_rows), chip_rows)

    @pl.loop(0, CHUNKS)
    def _(i):
        total = acc[i, mine, :]
        bulk(a2a.at[i, pl.ds(1, chips - 1)], a2a_send, a2a_recv.at[i], (dp, sibling)).wait_recv()
        for r in range(1, chips):
            total = total + a2a[i, r].astype(F32)
        low, high = total[:rows], total[rows:]
        at = pl.multiple_of(i * chunk, chunk)
        fin_out[:, pl.ds(at, chunk)] = jnp.where(core == 0, high, low)
        in_ref[:, pl.ds(pl.multiple_of(core * half + at, chunk), chunk)] = jnp.where(
            core == 0, low, high
        ).astype(BF16)

    fin = pltpu.make_async_remote_copy(
        src_ref=fin_out, dst_ref=fin_in, send_sem=fin_send, recv_sem=fin_recv,
        device_id=(dp, sibling), device_id_type=MESH,
    )
    fin.start()

    bulk(sib_out, half_send, half_recv.at[0], (dp, sibling)).wait_send()
    bulk(chip_sum.at[:, pl.ds(1, chips - 1)], a2a_send, a2a_recv.at[0], (dp, sibling)).wait_send()
    bulk(tok, sib_send, sib_recv.at[0, 0], (dp, sibling)).wait_send()
    bulk(tok.at[0, pl.ds(0, 2 * chips - 6)], x_send, x_recv.at[0], (1 - dp, col)).wait_send()
    bulk(tok.at[:, pl.ds(0, chips + 2)], ring_send, ring_recv.at[0, 0, 0], (dp, right)).wait_send()
    fin.wait()
    in_ref[:, pl.ds(pl.multiple_of((1 - core) * half, half), half)] = fin_in[...].astype(BF16)


def kernel_shards(n_cols, tokens, cotangent, block_weights, slot_block, slot_target, counts):
    n_slots, width = block_weights.shape[:2]
    n_dp = 2
    part = width // n_dp
    rows, features = tokens.shape
    n_f = features // width
    hidden_blocks = n_slots // SPC
    hidden = hidden_blocks * width
    places = 3 * hidden_blocks * n_f
    chips = n_cols // 2
    group_rows = rows * n_cols
    half = features // 2
    dma = pltpu.SemaphoreType.DMA
    vmem = pl.BlockSpec(memory_space=pltpu.VMEM)
    smem = pl.BlockSpec(memory_space=pltpu.SMEM)
    hbm = pl.BlockSpec(memory_space=pl.ANY)
    table_shape = (places // LANES + n_slots // LANES, LANES)
    slot_rows = (n_slots // LANES, LANES)
    return pl.pallas_call(
        functools.partial(layer_kernel, n_cols),
        out_shape=(
            pltpu.VMEM((rows, features), BF16),
            pltpu.VMEM((n_slots, part, width), BF16),
        ),
        in_specs=[smem, vmem, vmem, hbm, hbm, hbm],
        out_specs=(vmem, vmem),
        scratch_shapes=[
            pltpu.VMEM((n_dp, n_cols, rows, features), BF16),
            pltpu.VMEM((n_dp, n_cols, rows, features), BF16),
            pltpu.VMEM((places + 1, part, width), BF16),
            pltpu.VMEM((features, 2 * hidden), BF16),
            pltpu.VMEM((hidden, features), BF16),
            pltpu.VMEM((n_dp, group_rows, 2 * hidden), BF16),
            pltpu.VMEM((n_dp, group_rows, hidden), BF16),
            pltpu.VMEM((CHUNKS, group_rows, half // CHUNKS), F32),
            pltpu.VMEM((CHUNKS, group_rows, half // CHUNKS), BF16),
            pltpu.VMEM((CHUNKS, group_rows, half // CHUNKS), BF16),
            pltpu.VMEM((CHUNKS, chips, group_rows // chips, half // CHUNKS), BF16),
            pltpu.VMEM((CHUNKS, chips, group_rows // chips, half // CHUNKS), BF16),
            pltpu.VMEM((rows, half), F32),
            pltpu.VMEM((rows, half), F32),
            pltpu.VMEM((4 * part, n_dp * group_rows), BF16),
            pltpu.VMEM((hidden // n_dp, n_dp * group_rows), BF16),
            pltpu.VMEM(table_shape, jnp.int32),
            pltpu.SMEM(table_shape, jnp.int32),
            dma, dma((2,)), dma,
            dma, dma((chips // 2 + 2, 2, 4)),
            dma, dma((2, 2)),
            dma, dma((chips,)), dma, dma((CHUNKS,)),
            dma, dma((CHUNKS,)), dma, dma,
        ],
        compiler_params=pltpu.CompilerParams(
            collective_id=0, has_side_effects=True, vmem_limit_bytes=VMEM_LIMIT
        ),
    )(
        counts, slot_target.reshape(slot_rows), slot_block.reshape(slot_rows), tokens, cotangent,
        block_weights.reshape(n_slots * n_dp, part, width),
    )


def solution(mesh):
    n_dp, n_cols = mesh.shape["dp"], mesh.shape["cols"]
    paired = n_dp == 2 and n_cols % 4 == 0 and n_cols > 12

    def body(*args):
        tokens, weights = args[0], args[2]
        if paired and tokens.shape[0] % 16 == 0 and weights.shape[0] % LANES == 0 and weights.shape[0] // SPC % (n_cols // 4) == 0:
            return kernel_shards(n_cols, *args)
        return shards(*args)

    return jax.shard_map(
        body,
        mesh=mesh,
        in_specs=(
            P(("dp", "cols"), None),
            P(("dp", "cols"), None),
            P("cols", None, None),
            P("cols"),
            P("cols"),
            P("cols"),
        ),
        out_specs=(P(("dp", "cols"), None), P("cols", "dp", None)),
        check_vma=False,
    )
```

```python
import functools

import jax
import jax.numpy as jnp
from jax import lax
from jax.experimental import pallas as pl
from jax.experimental.pallas import tpu as pltpu
from jax.sharding import PartitionSpec as P

SPC = 32


def block_inputs(grad_rows, weights, block_select):
    partial_rows = jnp.einsum(
        "rsj,skj->rsk", grad_rows, weights, preferred_element_type=jnp.float32
    )
    summed = jnp.einsum("rsk,sb->rbk", partial_rows, block_select)
    return summed.reshape(summed.shape[0], summed.shape[1] * summed.shape[2])


def shards(tokens, cotangent, block_weights, slot_block, slot_target, counts):
    slot_total = block_weights.shape[0]
    block_width = block_weights.shape[1]
    columns = slot_total // SPC
    features = tokens.shape[1]
    block_count = features // block_width
    tokens_all, cot_all = (
        lax.all_gather(tokens, "cols", axis=0, tiled=True),
        lax.all_gather(cotangent, "cols", axis=0, tiled=True),
    )
    row_total = tokens_all.shape[0]
    live_slot = jnp.arange(slot_total) < counts[0]
    slot_kind = slot_target // columns
    places = slot_target % columns
    up_mask = (live_slot & (slot_kind < 2))[:, None].astype(jnp.float32)
    down_mask = (live_slot & (slot_kind == 2))[:, None].astype(jnp.float32)
    select_up = jax.nn.one_hot(slot_target, 2 * columns, dtype=jnp.float32) * up_mask
    select_down = jax.nn.one_hot(places, columns, dtype=jnp.float32) * down_mask
    block_select = jax.nn.one_hot(slot_block, block_count, dtype=jnp.float32)
    tokens_slots = jnp.take(
        tokens_all.reshape(row_total, block_count, block_width), slot_block, axis=1
    )
    products = jnp.einsum(
        "rsk,skj->rsj", tokens_slots, block_weights, preferred_element_type=jnp.float32
    )
    gate_up = jnp.einsum("rsj,sc->rcj", products, select_up)
    gate_pre = gate_up[:, :columns]
    up_pre = gate_up[:, columns:]
    sigmoid_gate = jax.nn.sigmoid(gate_pre)
    silu_gate = gate_pre * sigmoid_gate
    hidden = (silu_gate * up_pre).astype(jnp.bfloat16)
    cot_slots = jnp.take(cot_all.reshape(row_total, block_count, block_width), slot_block, axis=1)
    back_products = jnp.einsum(
        "rsj,skj->rsk", cot_slots, block_weights, preferred_element_type=jnp.float32
    )
    hidden_grad = jnp.einsum("rsk,sc->rck", back_products, select_down)
    gate_grad = (
        hidden_grad * up_pre * sigmoid_gate * (1.0 + gate_pre * (1.0 - sigmoid_gate))
    ).astype(jnp.bfloat16)
    up_grad = (hidden_grad * silu_gate).astype(jnp.bfloat16)
    pre_grad = jnp.concatenate([gate_grad, up_grad], axis=1)
    slot_grad = jnp.einsum(
        "rck,sc->rsk", pre_grad, select_up.astype(jnp.bfloat16), preferred_element_type=jnp.float32
    ).astype(jnp.bfloat16)
    slot_hidden = jnp.einsum(
        "rck,sc->rsk", hidden, select_down.astype(jnp.bfloat16), preferred_element_type=jnp.float32
    ).astype(jnp.bfloat16)
    weight_terms = jnp.einsum(
        "rsk,rsj->skj", tokens_slots, slot_grad, preferred_element_type=jnp.float32
    )
    weight_terms = weight_terms + jnp.einsum(
        "rsk,rsj->skj", slot_hidden, cot_slots, preferred_element_type=jnp.float32
    )
    input_terms = block_inputs(slot_grad, block_weights, block_select)
    input_sum = lax.psum_scatter(input_terms, "cols", scatter_dimension=0, tiled=True)
    input_grad = input_sum.astype(jnp.bfloat16)
    weight_sum = lax.psum_scatter(
        weight_terms.astype(jnp.bfloat16), "dp", scatter_dimension=1, tiled=True
    )
    return (input_grad, weight_sum)


MESH = pl.DeviceIdType.MESH
F32 = jnp.float32
BF16 = jnp.bfloat16
NT = (((1,), (1,)), ((), ()))
CHUNKS = 4
GROUP = 4
OUT_CUTS = 8
COPY_LIMIT = 1 << 20
VMEM_LIMIT = 60817408
LANES = 128


def layer_kernel(
    n_cols, count_ref, target_ref, block_ref, tok_ref, cot_ref, w_ref, in_ref, out_ref,
    tok, cot, blocks, wgu, wd, grads, hid, acc, sib_out, sib_in, pair_out, pair_in, line_out, line_in,
    fin_out, fin_in, lhs, hid_t, slots, table_rows, table_ref,
    w_sem, own_sem, slot_sem, table_sem, ring_send, ring_recv, sib_send, sib_recv,
    x_send, x_recv, half_send, half_recv, pair_send, pair_recv, line_send, line_recv, fin_send, fin_recv,
):
    chips = n_cols // 2
    steps = chips // 2
    rows = tok_ref.shape[0]
    group_rows = rows * n_cols
    features = tok_ref.shape[1]
    width = blocks.shape[2]
    part = blocks.shape[1]
    n_f = features // width
    hidden = wd.shape[0]
    n_h = hidden // width
    zero_at = blocks.shape[0] - 1
    pieces = width // part
    dead = w_ref.shape[0]
    table_size = zero_at // LANES
    n_slots = out_ref.shape[0]
    half = features // 2
    dp = lax.axis_index("dp")
    col = lax.axis_index("cols")
    core = col % 2
    chip = col // 2
    place = jnp.where(chip % 2 == 0, chip // 2, chips - 1 - chip // 2)

    def chip_at(p):
        p = (p + 2 * chips) % chips
        return jnp.where(p < steps, 2 * p, 2 * (chips - 1 - p) + 1)

    right = chip_at(place + 1) * 2 + core
    left = chip_at(place - 1) * 2 + core
    sibling = chip * 2 + 1 - core
    sides = ((tok_ref, tok), (cot_ref, cot))

    slot_copies = [
        pltpu.make_async_copy(ref, slots.at[a], slot_sem.at[a]) for a, ref in enumerate((target_ref, block_ref))
    ]
    for copy in slot_copies:
        copy.start()
    owns = [pltpu.make_async_copy(sides[a][0], sides[a][1].at[0, col], own_sem.at[a]) for a in range(2)]
    for own in owns:
        own.start()
    w_copy = pltpu.make_async_copy(w_ref, blocks.at[pl.ds(0, w_ref.shape[0])], w_sem)
    barrier = pltpu.get_barrier_semaphore()
    for r in range(1, chips):
        pl.semaphore_signal(barrier, inc=1, device_id=(dp, ((chip + r) % chips) * 2 + core), device_id_type=MESH)
    pl.semaphore_signal(barrier, inc=1, device_id=(dp, sibling), device_id_type=MESH)
    pl.semaphore_signal(barrier, inc=1, device_id=(1 - dp, col), device_id_type=MESH)
    pl.semaphore_wait(barrier, chips + 1)

    def piece(g, origin, a):
        at = pl.ds((a % 2) * half, half)
        return sides[a // 2][1].at[g, origin * 2 + core, :, at]

    def ring_copy(g, origin, direction, s, a):
        block = piece(g, origin, a)
        return pltpu.make_async_remote_copy(
            src_ref=block, dst_ref=block,
            send_sem=ring_send, recv_sem=ring_recv.at[g * steps + s, direction, a],
            device_id=(dp, right if direction == 0 else left), device_id_type=MESH,
        )

    def ring(g, direction, s, a):
        return ring_copy(g, chip_at(place - s if direction == 0 else place + s), direction, s, a)

    def ring_arrival(g, direction, s, a):
        return ring_copy(g, chip_at(place - 1 - s if direction == 0 else place + 1 + s), direction, s, a)

    def share_copy(g, k, a, lane):
        at = pl.ds((a % 2) * half, half)
        block = sides[a // 2][1].at[g, chip_at(place - k) * 2 + lane, :, at]
        return pltpu.make_async_remote_copy(
            src_ref=block, dst_ref=block,
            send_sem=sib_send, recv_sem=sib_recv.at[g, a // 2],
            device_id=(dp, sibling), device_id_type=MESH,
        )

    def share(g, k, a):
        return share_copy(g, k, a, core)

    def cross(k, a):
        origin = chip_at(place - k)
        return pltpu.make_async_remote_copy(
            src_ref=piece(0, origin, a), dst_ref=piece(1, origin, a),
            send_sem=x_send, recv_sem=x_recv.at[k],
            device_id=(1 - dp, col), device_id_type=MESH,
        )

    def piece_of(arr, direction, far):
        return 2 * arr + (direction if far else 1 - direction)

    def send(g, arr, s, far):
        for direction in range(2):
            ring(g, direction, s, piece_of(arr, direction, far)).start()

    def arrive(arr, s, far, forward):
        for direction in range(2):
            a = piece_of(arr, direction, far)
            ring_arrival(0, direction, s, a).wait_recv()
            if forward and s < (steps - 1 if far else steps - 2):
                ring(0, direction, s + 1, a).start()
            k = 1 + s if direction == 0 else chips - 1 - s
            share(0, k, a).start()
            if s > 1 or (s == 1 and not far):
                cross(k, a).start()

    def passed(s, far):
        arrive(1, s, far, True)

    def arrive_other(s, far):
        for direction in range(2):
            for arr in range(2):
                a = piece_of(arr, direction, far)
                ring_arrival(1, direction, s, a).wait_recv()
                if far and s == 0:
                    ring(1, direction, 1, a).start()
                share(1, 1 + s if direction == 0 else chips - 1 - s, a).start()

    def bulk(ref, send_sem, recv_sem, device):
        return pltpu.make_async_remote_copy(
            src_ref=ref, dst_ref=ref, send_sem=send_sem, recv_sem=recv_sem,
            device_id=device, device_id_type=MESH,
        )

    def all_shared(g, arr):
        bulk(sides[arr][1].at[g, pl.ds(0, chips)], sib_send, sib_recv.at[g, arr], (dp, sibling)).wait_recv()

    def cross_arrival(k, count=2):
        bulk(tok.at[1, pl.ds(0, count)], x_send, x_recv.at[k], (1 - dp, col)).wait_recv()

    def crossed(k, pieces=range(4)):
        cross_arrival(k, len(pieces) // 2)
        for a in pieces:
            share(1, k, a).start()

    for own in owns:
        own.wait()
    w_copy.start()
    send(0, 0, 0, True)
    send(0, 0, 0, False)
    send(0, 1, 0, True)
    for a in range(4):
        cross(0, a).start()
        share(0, 0, a).start()

    for copy in slot_copies:
        copy.wait()
    slot_place = slots[0] * n_f + slots[1]
    number = lax.broadcasted_iota(jnp.int32, slot_place.shape, 0) * LANES + lax.broadcasted_iota(
        jnp.int32, slot_place.shape, 1
    )
    live = number < count_ref[...]
    slot_place = jnp.where(live, slot_place, -1)
    table_rows[table_size:, :] = jnp.where(live, slot_place, zero_at)
    lane = lax.broadcasted_iota(jnp.int32, (LANES, LANES), 1)
    in_row = lax.broadcasted_iota(jnp.int32, (LANES, LANES), 0)
    columns = [
        jnp.broadcast_to(slot_place[j:j + 1], (LANES, LANES)).T for j in range(slot_place.shape[0])
    ]
    for t in range(table_size):
        row = jnp.zeros((1, LANES), jnp.int32)
        for j, column in enumerate(columns):
            hit = column == lane + t * LANES
            row = row + jnp.sum(
                jnp.where(hit, pieces * (in_row + j * LANES) - dead, 0), axis=0, keepdims=True
            )
        table_rows[t:t + 1, :] = row + dead
    table_copy = pltpu.make_async_copy(table_rows, table_ref, table_sem)
    table_copy.start()
    for at in [zero_at] + list(range(dead, dead + pieces)):
        blocks[at] = jnp.zeros((part, width), BF16)
    w_copy.wait()
    table_copy.wait()

    def spread(h, f):
        at = pl.multiple_of(f * width, width)
        hid_at = h * width
        for k in range(3):
            row, lane = divmod((k * n_h + h) * n_f, LANES)
            base = table_ref[row, lane + f]
            for piece in range(pieces):
                value = blocks[base + piece]
                if k < 2:
                    wgu[pl.ds(pl.multiple_of(at + piece * part, part), part),
                        pl.ds(k * hidden + hid_at, width)] = value
                else:
                    wd[pl.ds(hid_at + piece * part, part), pl.ds(at, width)] = value

    per_step = n_h // steps

    waiting = [(s, far) for s in range(steps) for far in (True, False) if far or s < steps - 1]
    for s in range(steps):
        if s == steps - 1:
            passed(*waiting.pop(0))
        arrive(0, s, True, True)
        if s < steps - 1:
            arrive(0, s, False, True)
        if s == 0:
            send(0, 1, 0, False)
        elif s < steps - 1:
            passed(*waiting.pop(0))
        if s < steps - 1:
            for u in range(2 * steps * s // (steps - 1), 2 * steps * (s + 1) // (steps - 1)):
                @pl.loop(u % 2 * n_f // 2, (u % 2 + 1) * n_f // 2, unroll=4)
                def _(f):
                    for j in range(per_step):
                        spread(u // 2 * per_step + j, f)

    all_shared(0, 0)
    span = hidden // steps

    def before(g, n):
        at = pl.multiple_of(n * span, span)
        x = tok[g].reshape(group_rows, features)
        gate = jnp.dot(x, wgu[:, pl.ds(at, span)], preferred_element_type=F32)
        up = jnp.dot(x, wgu[:, pl.ds(pl.multiple_of(hidden + at, span), span)], preferred_element_type=F32)
        return gate, up

    def after(g, n, gate, up):
        at = pl.multiple_of(n * span, span)
        back = lax.dot_general(
            cot[g].reshape(group_rows, features), wd[pl.ds(at, span), :], NT, preferred_element_type=F32
        )
        sig = jax.nn.sigmoid(gate)
        silu = gate * sig
        hid[g, :, pl.ds(at, span)] = (silu * up).astype(BF16)
        grads[g, :, pl.ds(at, span)] = (back * up * sig * (1.0 + gate * (1.0 - sig))).astype(BF16)
        grads[g, :, pl.ds(pl.multiple_of(hidden + at, span), span)] = (back * silu).astype(BF16)

    for s in range(steps):
        gate, up = before(0, s)
        acc[s, :, :span] = gate
        acc[s, :, span:] = up
        passed(*waiting.pop(0))
        if s == steps - 3:
            cross_arrival(0)
            for far in (True, False):
                for arr in range(2):
                    send(1, arr, 0, far)
            for a in range(4):
                share(1, 0, a).start()

    all_shared(0, 1)

    @pl.loop(0, steps)
    def _(s):
        after(0, s, acc[s, :, :span], acc[s, :, span:])

    crossed(2, (1, 3))
    crossed(chips - 2, (0, 2))
    arrive_other(0, True)

    chunk = half // CHUNKS
    chip_rows = group_rows // chips

    def terms(at):
        return lax.dot_general(grads[0], wgu[pl.ds(at, chunk), :], NT, preferred_element_type=F32)

    def to_sibling(i):
        return pltpu.make_async_remote_copy(
            src_ref=sib_out.at[i], dst_ref=sib_in.at[i], send_sem=half_send, recv_sem=half_recv.at[i],
            device_id=(dp, sibling), device_id_type=MESH,
        )

    lines = chips // 2
    line, side = chip // 2, chip % 2

    def rows_of(zz, yy):
        return pl.ds(pl.multiple_of((2 * zz + yy) * chip_rows, chip_rows), chip_rows)

    def to_partner(i):
        return pltpu.make_async_remote_copy(
            src_ref=pair_out.at[i], dst_ref=pair_in.at[i], send_sem=pair_send, recv_sem=pair_recv.at[i],
            device_id=(dp, (2 * line + 1 - side) * 2 + core), device_id_type=MESH,
        )

    def along_line(r, i):
        other = (line + r) % lines
        return pltpu.make_async_remote_copy(
            src_ref=line_out.at[i, other], dst_ref=line_in.at[i, r],
            send_sem=line_send, recv_sem=line_recv.at[i],
            device_id=(dp, (2 * other + side) * 2 + core), device_id_type=MESH,
        )

    def pair_sum(i):
        to_sibling(i).wait_recv()

        @pl.loop(0, lines)
        def _(zz):
            at = rows_of(zz, 1 - side)
            pair_out[i, zz] = (acc[i, at, :] + sib_in[i, at, :].astype(F32)).astype(BF16)

        to_partner(i).start()

        @pl.loop(0, lines)
        def _(zz):
            at = rows_of(zz, side)
            acc[i, at, :] = acc[i, at, :] + sib_in[i, at, :].astype(F32)

    def line_sum(i):
        to_partner(i).wait_recv()

        @pl.loop(0, lines)
        def _(zz):
            at = rows_of(zz, side)
            total = acc[i, at, :] + pair_in[i, zz].astype(F32)
            acc[i, at, :] = total
            line_out[i, zz] = total.astype(BF16)

        for r in range(1, lines):
            along_line(r, i).start()

    @pl.loop(0, CHUNKS)
    def _(i):
        at = pl.multiple_of(i * chunk, chunk)
        sib_out[i] = terms(pl.multiple_of((1 - core) * half + at, chunk)).astype(BF16)
        to_sibling(i).start()
        acc[i] = terms(pl.multiple_of(core * half + at, chunk))

        @pl.when(i > 0)
        def _():
            pair_sum(i - 1)

        @pl.when(i == 0)
        def _():
            arrive_other(0, False)

        @pl.when(i == CHUNKS - 3)
        def _():
            crossed(3)
            crossed(chips - 3)

        @pl.when(i == CHUNKS - 2)
        def _():
            arrive_other(1, True)
            for k in range(4, chips - 3):
                crossed(k)

    all_shared(1, 0)
    all_shared(1, 1)

    @pl.loop(0, steps)
    def _(s):
        gate, up = before(1, s)
        after(1, s, gate, up)

        @pl.when(s == 0)
        def _():
            pair_sum(CHUNKS - 1)
            line_sum(0)

        @pl.when(s >= 2)
        def _():
            line_sum(s - 1)

    def take_part(block):
        out = block[:part]
        for i in range(1, width // part):
            out = jnp.where(dp == i, block[i * part:(i + 1) * part], out)
        return out

    for g in range(2):
        for h in range(n_h):
            hid_t[pl.ds(h * part, part), pl.ds(g * group_rows, group_rows)] = take_part(
                hid[g, :, pl.ds(h * width, width)].T
            )
    four = GROUP
    mine = rows_of(line, side)
    fin = pltpu.make_async_remote_copy(
        src_ref=fin_out, dst_ref=fin_in, send_sem=fin_send, recv_sem=fin_recv,
        device_id=(dp, sibling), device_id_type=MESH,
    )

    def final_sum(i):
        total = acc[i, mine, :]
        bulk(line_in.at[i, pl.ds(1, lines - 1)], line_send, line_recv.at[i], (dp, sibling)).wait_recv()
        for r in range(1, lines):
            total = total + line_in[i, r].astype(F32)
        low, high = total[:rows], total[rows:]
        at = pl.multiple_of(i * chunk, chunk)
        fin_out[:, pl.ds(at, chunk)] = jnp.where(core == 0, high, low)
        in_ref[:, pl.ds(pl.multiple_of(core * half + at, chunk), chunk)] = jnp.where(
            core == 0, low, high
        ).astype(BF16)

    tiles = n_f // four

    def prepare(i, slot):
        at = jnp.minimum(i, tiles - 1) * four * width
        for g in range(2):
            for b in range(four):
                piece = tok[g, :, :, pl.ds(pl.multiple_of(at + b * width, width), width)]
                lhs[slot, pl.ds(b * part, part), pl.ds(g * group_rows, group_rows)] = take_part(
                    piece.reshape(group_rows, width).T
                )

    def tile_grads(i, slot):
        for n in range(2 * n_h // 4):
            cut = slice(n * 4 * width, (n + 1) * 4 * width)
            out = jnp.dot(
                lhs[slot], grads[:, :, cut].reshape(2 * group_rows, 4 * width), preferred_element_type=F32
            ).astype(BF16)
            for h in range(4):
                for b in range(four):
                    blocks[(n * 4 + h) * n_f + i * four + b] = out[
                        b * part:(b + 1) * part, h * width:(h + 1) * width
                    ]
            if n == 0:
                prepare(i + 1, 1 - slot)
        c = cot[:, :, :, pl.ds(pl.multiple_of(i * four * width, width), four * width)]
        out = jnp.dot(
            hid_t[...], c.reshape(2 * group_rows, four * width), preferred_element_type=F32
        ).astype(BF16)
        for h in range(n_h):
            for b in range(four):
                blocks[(2 * n_h + h) * n_f + i * four + b] = out[
                    h * part:(h + 1) * part, b * width:(b + 1) * width
                ]

    prepare(0, 0)

    @pl.loop(0, tiles // 2)
    def _(p):
        tile_grads(2 * p, 0)

        @pl.when(p == 0)
        def _():
            line_sum(CHUNKS - 1)

        @pl.when(p == tiles // 2 - 1)
        def _():
            @pl.loop(0, CHUNKS)
            def _(n):
                final_sum(n)

            fin.start()

        tile_grads(2 * p + 1, 1)

    for r in range(n_slots // LANES):
        @pl.loop(0, LANES, unroll=8)
        def _(j):
            out_ref[r * LANES + j] = blocks[table_ref[table_size + r, j]]

    bulk(sib_out, half_send, half_recv.at[0], (dp, sibling)).wait_send()
    bulk(pair_out, pair_send, pair_recv.at[0], (dp, sibling)).wait_send()
    bulk(line_out.at[:, pl.ds(1, lines - 1)], line_send, line_recv.at[0], (dp, sibling)).wait_send()
    bulk(tok, sib_send, sib_recv.at[0, 0], (dp, sibling)).wait_send()
    bulk(tok.at[0, pl.ds(0, 2 * chips - 6)], x_send, x_recv.at[0], (1 - dp, col)).wait_send()
    bulk(tok.at[:, pl.ds(0, chips + 2)], ring_send, ring_recv.at[0, 0, 0], (dp, right)).wait_send()
    fin.wait()
    in_ref[:, pl.ds(pl.multiple_of((1 - core) * half, half), half)] = fin_in[...].astype(BF16)


def out_kernel(in_ref, wg_ref, in_out, wg_out, in_sem, wg_sem):
    per_cut = wg_ref.shape[0] // OUT_CUTS
    first = pltpu.make_async_copy(in_ref, in_out, in_sem)
    first.start()
    for c in range(OUT_CUTS):
        at = pl.ds(c * per_cut, per_cut)
        pltpu.make_async_copy(wg_ref.at[at], wg_out.at[at], wg_sem).start()
    first.wait()
    pltpu.make_async_copy(wg_ref, wg_out, wg_sem).wait()


def kernel_shards(n_cols, tokens, cotangent, block_weights, slot_block, slot_target, counts):
    n_slots, width = block_weights.shape[:2]
    n_dp = 2
    part = width // n_dp
    rows, features = tokens.shape
    n_f = features // width
    hidden_blocks = n_slots // SPC
    hidden = hidden_blocks * width
    places = 3 * hidden_blocks * n_f
    chips = n_cols // 2
    group_rows = rows * n_cols
    half = features // 2
    dma = pltpu.SemaphoreType.DMA
    vmem = pl.BlockSpec(memory_space=pltpu.VMEM)
    hbm = pl.BlockSpec(memory_space=pl.ANY)
    table_shape = (places // LANES + n_slots // LANES, LANES)
    slot_rows = (n_slots // LANES, LANES)
    results = pl.pallas_call(
        functools.partial(layer_kernel, n_cols),
        out_shape=(
            pltpu.VMEM((rows, features), BF16),
            pltpu.VMEM((n_slots, part, width), BF16),
        ),
        in_specs=[vmem, hbm, hbm, hbm, hbm, hbm],
        out_specs=(vmem, vmem),
        scratch_shapes=[
            pltpu.VMEM((n_dp, n_cols, rows, features), BF16),
            pltpu.VMEM((n_dp, n_cols, rows, features), BF16),
            pltpu.VMEM((places + 1, part, width), BF16),
            pltpu.VMEM((features, 2 * hidden), BF16),
            pltpu.VMEM((hidden, features), BF16),
            pltpu.VMEM((n_dp, group_rows, 2 * hidden), BF16),
            pltpu.VMEM((n_dp, group_rows, hidden), BF16),
            pltpu.VMEM((CHUNKS, group_rows, half // CHUNKS), F32),
            pltpu.VMEM((CHUNKS, group_rows, half // CHUNKS), BF16),
            pltpu.VMEM((CHUNKS, group_rows, half // CHUNKS), BF16),
            pltpu.VMEM((CHUNKS, chips // 2, group_rows // chips, half // CHUNKS), BF16),
            pltpu.VMEM((CHUNKS, chips // 2, group_rows // chips, half // CHUNKS), BF16),
            pltpu.VMEM((CHUNKS, chips // 2, group_rows // chips, half // CHUNKS), BF16),
            pltpu.VMEM((CHUNKS, chips // 2, group_rows // chips, half // CHUNKS), BF16),
            pltpu.VMEM((rows, half), F32),
            pltpu.VMEM((rows, half), F32),
            pltpu.VMEM((2, GROUP * part, n_dp * group_rows), BF16),
            pltpu.VMEM((hidden // n_dp, n_dp * group_rows), BF16),
            pltpu.VMEM((2,) + slot_rows, jnp.int32),
            pltpu.VMEM(table_shape, jnp.int32),
            pltpu.SMEM(table_shape, jnp.int32),
            dma, dma((2,)), dma((2,)), dma,
            dma, dma((chips // 2 + 2, 2, 4)),
            dma, dma((2, 2)),
            dma, dma((chips,)), dma, dma((CHUNKS,)),
            dma, dma((CHUNKS,)), dma, dma((CHUNKS,)), dma, dma,
        ],
        compiler_params=pltpu.CompilerParams(
            collective_id=0, has_side_effects=True, vmem_limit_bytes=VMEM_LIMIT
        ),
    )(
        counts.reshape(1, 1), slot_target.reshape(slot_rows), slot_block.reshape(slot_rows), tokens, cotangent,
        block_weights.reshape(n_slots * n_dp, part, width),
    )
    return pl.pallas_call(
        out_kernel,
        out_shape=(
            jax.ShapeDtypeStruct((rows, features), BF16),
            jax.ShapeDtypeStruct((n_slots, part, width), BF16),
        ),
        in_specs=[vmem, vmem],
        out_specs=(hbm, hbm),
        scratch_shapes=[dma, dma],
        compiler_params=pltpu.CompilerParams(vmem_limit_bytes=COPY_LIMIT),
    )(*results)


def solution(mesh):
    n_dp, n_cols = mesh.shape["dp"], mesh.shape["cols"]
    paired = n_dp == 2 and n_cols == 4 * CHUNKS

    def body(*args):
        tokens, weights = args[0], args[2]
        if paired and tokens.shape[0] % 16 == 0 and weights.shape[0] % LANES == 0 and LANES * weights.shape[1] % tokens.shape[1] == 0 and weights.shape[0] // SPC % (n_cols // 4) == 0:
            return kernel_shards(n_cols, *args)
        return shards(*args)

    return jax.shard_map(
        body,
        mesh=mesh,
        in_specs=(
            P(("dp", "cols"), None),
            P(("dp", "cols"), None),
            P("cols", None, None),
            P("cols"),
            P("cols"),
            P("cols"),
        ),
        out_specs=(P(("dp", "cols"), None), P("cols", "dp", None)),
        check_vma=False,
    )
```

```python
import functools

import jax
import jax.numpy as jnp
from jax import lax
from jax.experimental import pallas as pl
from jax.experimental.pallas import tpu as pltpu
from jax.sharding import PartitionSpec as P

SPC = 32


def block_inputs(grad_rows, weights, block_select):
    partial_rows = jnp.einsum(
        "rsj,skj->rsk", grad_rows, weights, preferred_element_type=jnp.float32
    )
    summed = jnp.einsum("rsk,sb->rbk", partial_rows, block_select)
    return summed.reshape(summed.shape[0], summed.shape[1] * summed.shape[2])


def shards(tokens, cotangent, block_weights, slot_block, slot_target, counts):
    slot_total = block_weights.shape[0]
    block_width = block_weights.shape[1]
    columns = slot_total // SPC
    features = tokens.shape[1]
    block_count = features // block_width
    tokens_all, cot_all = (
        lax.all_gather(tokens, "cols", axis=0, tiled=True),
        lax.all_gather(cotangent, "cols", axis=0, tiled=True),
    )
    row_total = tokens_all.shape[0]
    live_slot = jnp.arange(slot_total) < counts[0]
    slot_kind = slot_target // columns
    places = slot_target % columns
    up_mask = (live_slot & (slot_kind < 2))[:, None].astype(jnp.float32)
    down_mask = (live_slot & (slot_kind == 2))[:, None].astype(jnp.float32)
    select_up = jax.nn.one_hot(slot_target, 2 * columns, dtype=jnp.float32) * up_mask
    select_down = jax.nn.one_hot(places, columns, dtype=jnp.float32) * down_mask
    block_select = jax.nn.one_hot(slot_block, block_count, dtype=jnp.float32)
    tokens_slots = jnp.take(
        tokens_all.reshape(row_total, block_count, block_width), slot_block, axis=1
    )
    products = jnp.einsum(
        "rsk,skj->rsj", tokens_slots, block_weights, preferred_element_type=jnp.float32
    )
    gate_up = jnp.einsum("rsj,sc->rcj", products, select_up)
    gate_pre = gate_up[:, :columns]
    up_pre = gate_up[:, columns:]
    sigmoid_gate = jax.nn.sigmoid(gate_pre)
    silu_gate = gate_pre * sigmoid_gate
    hidden = (silu_gate * up_pre).astype(jnp.bfloat16)
    cot_slots = jnp.take(cot_all.reshape(row_total, block_count, block_width), slot_block, axis=1)
    back_products = jnp.einsum(
        "rsj,skj->rsk", cot_slots, block_weights, preferred_element_type=jnp.float32
    )
    hidden_grad = jnp.einsum("rsk,sc->rck", back_products, select_down)
    gate_grad = (
        hidden_grad * up_pre * sigmoid_gate * (1.0 + gate_pre * (1.0 - sigmoid_gate))
    ).astype(jnp.bfloat16)
    up_grad = (hidden_grad * silu_gate).astype(jnp.bfloat16)
    pre_grad = jnp.concatenate([gate_grad, up_grad], axis=1)
    slot_grad = jnp.einsum(
        "rck,sc->rsk", pre_grad, select_up.astype(jnp.bfloat16), preferred_element_type=jnp.float32
    ).astype(jnp.bfloat16)
    slot_hidden = jnp.einsum(
        "rck,sc->rsk", hidden, select_down.astype(jnp.bfloat16), preferred_element_type=jnp.float32
    ).astype(jnp.bfloat16)
    weight_terms = jnp.einsum(
        "rsk,rsj->skj", tokens_slots, slot_grad, preferred_element_type=jnp.float32
    )
    weight_terms = weight_terms + jnp.einsum(
        "rsk,rsj->skj", slot_hidden, cot_slots, preferred_element_type=jnp.float32
    )
    input_terms = block_inputs(slot_grad, block_weights, block_select)
    input_sum = lax.psum_scatter(input_terms, "cols", scatter_dimension=0, tiled=True)
    input_grad = input_sum.astype(jnp.bfloat16)
    weight_sum = lax.psum_scatter(
        weight_terms.astype(jnp.bfloat16), "dp", scatter_dimension=1, tiled=True
    )
    return (input_grad, weight_sum)


MESH = pl.DeviceIdType.MESH
F32 = jnp.float32
BF16 = jnp.bfloat16
NT = (((1,), (1,)), ((), ()))
CHUNKS = 4
GROUP = 4
OUT_CUTS = 8
COPY_LIMIT = 1 << 20
VMEM_LIMIT = 60817408
LANES = 128


def layer_kernel(
    n_cols, count_ref, target_ref, block_ref, tok_ref, cot_ref, w_ref, in_ref, out_ref,
    tok, cot, blocks, wgu, wd, grads, hid, acc, sib_out, sib_in, pair_out, pair_in, line_out, line_in,
    fin_out, fin_in, lhs, hid_t, slots, table_rows, table_ref,
    w_sem, own_sem, slot_sem, table_sem, ring_send, ring_recv, sib_send, sib_recv,
    x_send, x_recv, half_send, half_recv, pair_send, pair_recv, line_send, line_recv, fin_send, fin_recv,
):
    chips = n_cols // 2
    steps = chips // 2
    rows = tok_ref.shape[0]
    group_rows = rows * n_cols
    features = tok_ref.shape[1]
    width = blocks.shape[2]
    part = blocks.shape[1]
    n_f = features // width
    hidden = wd.shape[0]
    n_h = hidden // width
    zero_at = blocks.shape[0] - 1
    pieces = width // part
    dead = w_ref.shape[0]
    table_size = zero_at // LANES
    n_slots = out_ref.shape[0]
    half = features // 2
    dp = lax.axis_index("dp")
    col = lax.axis_index("cols")
    core = col % 2
    chip = col // 2
    place = jnp.where(chip % 2 == 0, chip // 2, chips - 1 - chip // 2)

    def chip_at(p):
        p = (p + 2 * chips) % chips
        return jnp.where(p < steps, 2 * p, 2 * (chips - 1 - p) + 1)

    right = chip_at(place + 1) * 2 + core
    left = chip_at(place - 1) * 2 + core
    sibling = chip * 2 + 1 - core
    sides = ((tok_ref, tok), (cot_ref, cot))

    slot_copies = [
        pltpu.make_async_copy(ref, slots.at[a], slot_sem.at[a]) for a, ref in enumerate((target_ref, block_ref))
    ]
    for copy in slot_copies:
        copy.start()
    owns = [pltpu.make_async_copy(sides[a][0], sides[a][1].at[0, col], own_sem.at[a]) for a in range(2)]
    for own in owns:
        own.start()
    w_copy = pltpu.make_async_copy(w_ref, blocks.at[pl.ds(0, w_ref.shape[0])], w_sem)
    barrier = pltpu.get_barrier_semaphore()
    for r in range(1, chips):
        pl.semaphore_signal(barrier, inc=1, device_id=(dp, ((chip + r) % chips) * 2 + core), device_id_type=MESH)
    pl.semaphore_signal(barrier, inc=1, device_id=(dp, sibling), device_id_type=MESH)
    pl.semaphore_signal(barrier, inc=1, device_id=(1 - dp, col), device_id_type=MESH)
    pl.semaphore_wait(barrier, chips + 1)

    def piece(g, origin, a):
        at = pl.ds((a % 2) * half, half)
        return sides[a // 2][1].at[g, origin * 2 + core, :, at]

    def ring_copy(g, origin, direction, s, a):
        block = piece(g, origin, a)
        return pltpu.make_async_remote_copy(
            src_ref=block, dst_ref=block,
            send_sem=ring_send, recv_sem=ring_recv.at[g * steps + s, direction, a],
            device_id=(dp, right if direction == 0 else left), device_id_type=MESH,
        )

    def ring(g, direction, s, a):
        return ring_copy(g, chip_at(place - s if direction == 0 else place + s), direction, s, a)

    def ring_arrival(g, direction, s, a):
        return ring_copy(g, chip_at(place - 1 - s if direction == 0 else place + 1 + s), direction, s, a)

    def share_copy(g, k, a, lane):
        at = pl.ds((a % 2) * half, half)
        block = sides[a // 2][1].at[g, chip_at(place - k) * 2 + lane, :, at]
        return pltpu.make_async_remote_copy(
            src_ref=block, dst_ref=block,
            send_sem=sib_send, recv_sem=sib_recv.at[g, a // 2],
            device_id=(dp, sibling), device_id_type=MESH,
        )

    def share(g, k, a):
        return share_copy(g, k, a, core)

    def cross(k, a):
        origin = chip_at(place - k)
        return pltpu.make_async_remote_copy(
            src_ref=piece(0, origin, a), dst_ref=piece(1, origin, a),
            send_sem=x_send, recv_sem=x_recv.at[k],
            device_id=(1 - dp, col), device_id_type=MESH,
        )

    def piece_of(arr, direction, far):
        return 2 * arr + (direction if far else 1 - direction)

    def send(g, arr, s, far):
        for direction in range(2):
            ring(g, direction, s, piece_of(arr, direction, far)).start()

    def arrive(arr, s, far, forward):
        for direction in range(2):
            a = piece_of(arr, direction, far)
            ring_arrival(0, direction, s, a).wait_recv()
            if forward and s < (steps - 1 if far else steps - 2):
                ring(0, direction, s + 1, a).start()
            k = 1 + s if direction == 0 else chips - 1 - s
            share(0, k, a).start()
            if s > 1 or (s == 1 and not far):
                cross(k, a).start()

    def passed(s, far):
        arrive(1, s, far, True)

    def arrive_other(s, far):
        for direction in range(2):
            for arr in range(2):
                a = piece_of(arr, direction, far)
                ring_arrival(1, direction, s, a).wait_recv()
                if far and s == 0:
                    ring(1, direction, 1, a).start()
                share(1, 1 + s if direction == 0 else chips - 1 - s, a).start()

    def bulk(ref, send_sem, recv_sem, device):
        return pltpu.make_async_remote_copy(
            src_ref=ref, dst_ref=ref, send_sem=send_sem, recv_sem=recv_sem,
            device_id=device, device_id_type=MESH,
        )

    def all_shared(g, arr):
        bulk(sides[arr][1].at[g, pl.ds(0, chips)], sib_send, sib_recv.at[g, arr], (dp, sibling)).wait_recv()

    def cross_arrival(k, count=2):
        bulk(tok.at[1, pl.ds(0, count)], x_send, x_recv.at[k], (1 - dp, col)).wait_recv()

    def crossed(k, pieces=range(4)):
        cross_arrival(k, len(pieces) // 2)
        for a in pieces:
            share(1, k, a).start()

    for own in owns:
        own.wait()
    w_copy.start()
    send(0, 0, 0, True)
    send(0, 0, 0, False)
    send(0, 1, 0, True)
    for a in range(4):
        cross(0, a).start()
        share(0, 0, a).start()

    for copy in slot_copies:
        copy.wait()
    slot_place = slots[0] * n_f + slots[1]
    number = lax.broadcasted_iota(jnp.int32, slot_place.shape, 0) * LANES + lax.broadcasted_iota(
        jnp.int32, slot_place.shape, 1
    )
    live = number < count_ref[...]
    slot_place = jnp.where(live, slot_place, -1)
    table_rows[table_size:, :] = jnp.where(live, slot_place, zero_at)
    lane = lax.broadcasted_iota(jnp.int32, (LANES, LANES), 1)
    in_row = lax.broadcasted_iota(jnp.int32, (LANES, LANES), 0)
    columns = [
        jnp.broadcast_to(slot_place[j:j + 1], (LANES, LANES)).T for j in range(slot_place.shape[0])
    ]
    for t in range(table_size):
        row = jnp.zeros((1, LANES), jnp.int32)
        for j, column in enumerate(columns):
            hit = column == lane + t * LANES
            row = row + jnp.sum(
                jnp.where(hit, pieces * (in_row + j * LANES) - dead, 0), axis=0, keepdims=True
            )
        table_rows[t:t + 1, :] = row + dead
    table_copy = pltpu.make_async_copy(table_rows, table_ref, table_sem)
    table_copy.start()
    for at in [zero_at] + list(range(dead, dead + pieces)):
        blocks[at] = jnp.zeros((part, width), BF16)
    w_copy.wait()
    table_copy.wait()

    def spread(h, f):
        at = pl.multiple_of(f * width, width)
        hid_at = h * width
        for k in range(3):
            row, lane = divmod((k * n_h + h) * n_f, LANES)
            base = table_ref[row, lane + f]
            for piece in range(pieces):
                value = blocks[base + piece]
                if k < 2:
                    wgu[pl.ds(pl.multiple_of(at + piece * part, part), part),
                        pl.ds(k * hidden + hid_at, width)] = value
                else:
                    wd[pl.ds(hid_at + piece * part, part), pl.ds(at, width)] = value

    per_step = n_h // steps

    waiting = [(s, far) for s in range(steps) for far in (True, False) if far or s < steps - 1]
    for s in range(steps):
        if s == steps - 1:
            passed(*waiting.pop(0))
        arrive(0, s, True, True)
        if s < steps - 1:
            arrive(0, s, False, True)
        if s == 0:
            send(0, 1, 0, False)
        elif s < steps - 1:
            passed(*waiting.pop(0))
        if s < steps - 1:
            for u in range(2 * steps * s // (steps - 1), 2 * steps * (s + 1) // (steps - 1)):
                @pl.loop(u % 2 * n_f // 2, (u % 2 + 1) * n_f // 2, unroll=4)
                def _(f):
                    for j in range(per_step):
                        spread(u // 2 * per_step + j, f)

    all_shared(0, 0)
    span = hidden // steps

    def before(g, n):
        at = pl.multiple_of(n * span, span)
        x = tok[g].reshape(group_rows, features)
        gate = jnp.dot(x, wgu[:, pl.ds(at, span)], preferred_element_type=F32)
        up = jnp.dot(x, wgu[:, pl.ds(pl.multiple_of(hidden + at, span), span)], preferred_element_type=F32)
        return gate, up

    def after(g, n, gate, up):
        at = pl.multiple_of(n * span, span)
        back = lax.dot_general(
            cot[g].reshape(group_rows, features), wd[pl.ds(at, span), :], NT, preferred_element_type=F32
        )
        sig = jax.nn.sigmoid(gate)
        silu = gate * sig
        hid[g, :, pl.ds(at, span)] = (silu * up).astype(BF16)
        grads[g, :, pl.ds(at, span)] = (back * up * sig * (1.0 + gate * (1.0 - sig))).astype(BF16)
        grads[g, :, pl.ds(pl.multiple_of(hidden + at, span), span)] = (back * silu).astype(BF16)

    def take_part(block):
        out = block[:part]
        for i in range(1, width // part):
            out = jnp.where(dp == i, block[i * part:(i + 1) * part], out)
        return out

    def turn_hidden(g):
        for h in range(n_h):
            hid_t[pl.ds(h * part, part), pl.ds(g * group_rows, group_rows)] = take_part(
                hid[g, :, pl.ds(h * width, width)].T
            )

    for s in range(steps):
        gate, up = before(0, s)
        sig = jax.nn.sigmoid(gate)
        silu = gate * sig
        hid[0, :, s * span:(s + 1) * span] = (silu * up).astype(BF16)
        acc[s, :, :span] = up * sig * (1.0 + gate * (1.0 - sig))
        acc[s, :, span:] = silu
        passed(*waiting.pop(0))
        if s == steps - 3:
            cross_arrival(0)
            for far in (True, False):
                for arr in range(2):
                    send(1, arr, 0, far)
            for a in range(4):
                share(1, 0, a).start()

    turn_hidden(0)
    all_shared(0, 1)

    for s in range(steps):
        at = s * span
        back = lax.dot_general(
            cot[0].reshape(group_rows, features), wd[at:at + span, :], NT, preferred_element_type=F32
        )
        grads[0, :, at:at + span] = (back * acc[s, :, :span]).astype(BF16)
        grads[0, :, hidden + at:hidden + at + span] = (back * acc[s, :, span:]).astype(BF16)

    crossed(2, (1, 3))
    crossed(chips - 2, (0, 2))
    arrive_other(0, True)

    chunk = half // CHUNKS
    chip_rows = group_rows // chips

    def terms(at):
        return lax.dot_general(grads[0], wgu[pl.ds(at, chunk), :], NT, preferred_element_type=F32)

    def to_sibling(i):
        return pltpu.make_async_remote_copy(
            src_ref=sib_out.at[i], dst_ref=sib_in.at[i], send_sem=half_send, recv_sem=half_recv.at[i],
            device_id=(dp, sibling), device_id_type=MESH,
        )

    lines = chips // 2
    line, side = chip // 2, chip % 2

    def rows_of(zz, yy):
        return pl.ds(pl.multiple_of((2 * zz + yy) * chip_rows, chip_rows), chip_rows)

    def to_partner(i):
        return pltpu.make_async_remote_copy(
            src_ref=pair_out.at[i], dst_ref=pair_in.at[i], send_sem=pair_send, recv_sem=pair_recv.at[i],
            device_id=(dp, (2 * line + 1 - side) * 2 + core), device_id_type=MESH,
        )

    def along_line(r, i):
        other = (line + r) % lines
        return pltpu.make_async_remote_copy(
            src_ref=line_out.at[i, other], dst_ref=line_in.at[i, r],
            send_sem=line_send, recv_sem=line_recv.at[i],
            device_id=(dp, (2 * other + side) * 2 + core), device_id_type=MESH,
        )

    def pair_add(i):
        for zz in range(lines):
            at = rows_of(zz, 1 - side)
            pair_out[i, zz] = (acc[i, at, :] + sib_in[i, at, :].astype(F32)).astype(BF16)
        to_partner(i).start()
        for zz in range(lines):
            at = rows_of(zz, side)
            acc[i, at, :] = acc[i, at, :] + sib_in[i, at, :].astype(F32)

    def pair_sum(i):
        to_sibling(i).wait_recv()
        pair_add(i)

    def line_sum(i):
        to_partner(i).wait_recv()

        @pl.loop(0, lines)
        def _(zz):
            at = rows_of(zz, side)
            total = acc[i, at, :] + pair_in[i, zz].astype(F32)
            acc[i, at, :] = total
            line_out[i, zz] = total.astype(BF16)

        for r in range(1, lines):
            along_line(r, i).start()

    for i in range(CHUNKS):
        at = i * chunk
        sib_out[i] = terms(pl.multiple_of((1 - core) * half + at, chunk)).astype(BF16)
        to_sibling(i).start()
        if i > 0:
            to_sibling(i - 1).wait_recv()
        if i == CHUNKS - 1:
            arrive_other(1, True)
            for k in range(4, chips - 3):
                crossed(k)
        acc[i] = terms(pl.multiple_of(core * half + at, chunk))
        if i > 0:
            pair_add(i - 1)
        if i == 0:
            arrive_other(0, False)
        if i == CHUNKS - 2:
            crossed(3)
            crossed(chips - 3)

    all_shared(1, 0)
    all_shared(1, 1)

    @pl.loop(0, steps)
    def _(s):
        gate, up = before(1, s)
        after(1, s, gate, up)

        @pl.when(s == 0)
        def _():
            pair_sum(CHUNKS - 1)
            line_sum(0)

        @pl.when(s >= 2)
        def _():
            line_sum(s - 1)

    turn_hidden(1)
    four = GROUP
    mine = rows_of(line, side)
    fin = pltpu.make_async_remote_copy(
        src_ref=fin_out, dst_ref=fin_in, send_sem=fin_send, recv_sem=fin_recv,
        device_id=(dp, sibling), device_id_type=MESH,
    )

    def final_sum(i):
        total = acc[i, mine, :]
        bulk(line_in.at[i, pl.ds(1, lines - 1)], line_send, line_recv.at[i], (dp, sibling)).wait_recv()
        for r in range(1, lines):
            total = total + line_in[i, r].astype(F32)
        low, high = total[:rows], total[rows:]
        at = pl.multiple_of(i * chunk, chunk)
        fin_out[:, pl.ds(at, chunk)] = jnp.where(core == 0, high, low)
        in_ref[:, pl.ds(pl.multiple_of(core * half + at, chunk), chunk)] = jnp.where(
            core == 0, low, high
        ).astype(BF16)

    tiles = n_f // four

    def prepare(i, slot):
        at = jnp.minimum(i, tiles - 1) * four * width
        for g in range(2):
            for b in range(four):
                piece = tok[g, :, :, pl.ds(pl.multiple_of(at + b * width, width), width)]
                lhs[slot, pl.ds(b * part, part), pl.ds(g * group_rows, group_rows)] = take_part(
                    piece.reshape(group_rows, width).T
                )

    def tile_grads(i, slot):
        for n in range(2 * n_h // 4):
            cut = slice(n * 4 * width, (n + 1) * 4 * width)
            out = jnp.dot(
                lhs[slot], grads[:, :, cut].reshape(2 * group_rows, 4 * width), preferred_element_type=F32
            ).astype(BF16)
            for h in range(4):
                for b in range(four):
                    blocks[(n * 4 + h) * n_f + i * four + b] = out[
                        b * part:(b + 1) * part, h * width:(h + 1) * width
                    ]
            if n == 0:
                prepare(i + 1, 1 - slot)
        c = cot[:, :, :, pl.ds(pl.multiple_of(i * four * width, width), four * width)]
        out = jnp.dot(
            hid_t[...], c.reshape(2 * group_rows, four * width), preferred_element_type=F32
        ).astype(BF16)
        for h in range(n_h):
            for b in range(four):
                blocks[(2 * n_h + h) * n_f + i * four + b] = out[
                    h * part:(h + 1) * part, b * width:(b + 1) * width
                ]

    prepare(0, 0)

    @pl.loop(0, tiles // 2)
    def _(p):
        tile_grads(2 * p, 0)

        @pl.when(p == 0)
        def _():
            line_sum(CHUNKS - 1)

        @pl.when(p == tiles // 2 - 1)
        def _():
            @pl.loop(0, CHUNKS)
            def _(n):
                final_sum(n)

            fin.start()

        tile_grads(2 * p + 1, 1)

    for r in range(n_slots // LANES):
        @pl.loop(0, LANES, unroll=32)
        def _(j):
            out_ref[r * LANES + j] = blocks[table_ref[table_size + r, j]]

    bulk(sib_out, half_send, half_recv.at[0], (dp, sibling)).wait_send()
    bulk(pair_out, pair_send, pair_recv.at[0], (dp, sibling)).wait_send()
    bulk(line_out.at[:, pl.ds(1, lines - 1)], line_send, line_recv.at[0], (dp, sibling)).wait_send()
    bulk(tok, sib_send, sib_recv.at[0, 0], (dp, sibling)).wait_send()
    bulk(tok.at[0, pl.ds(0, 2 * chips - 6)], x_send, x_recv.at[0], (1 - dp, col)).wait_send()
    bulk(tok.at[:, pl.ds(0, chips + 2)], ring_send, ring_recv.at[0, 0, 0], (dp, right)).wait_send()
    fin.wait()
    in_ref[:, pl.ds(pl.multiple_of((1 - core) * half, half), half)] = fin_in[...].astype(BF16)


def out_kernel(in_ref, wg_ref, in_out, wg_out, in_sem, wg_sem):
    per_cut = wg_ref.shape[0] // OUT_CUTS
    first = pltpu.make_async_copy(in_ref, in_out, in_sem)
    first.start()
    for c in range(OUT_CUTS):
        at = pl.ds(c * per_cut, per_cut)
        pltpu.make_async_copy(wg_ref.at[at], wg_out.at[at], wg_sem).start()
    first.wait()
    pltpu.make_async_copy(wg_ref, wg_out, wg_sem).wait()


def kernel_shards(n_cols, tokens, cotangent, block_weights, slot_block, slot_target, counts):
    n_slots, width = block_weights.shape[:2]
    n_dp = 2
    part = width // n_dp
    rows, features = tokens.shape
    n_f = features // width
    hidden_blocks = n_slots // SPC
    hidden = hidden_blocks * width
    places = 3 * hidden_blocks * n_f
    chips = n_cols // 2
    group_rows = rows * n_cols
    half = features // 2
    dma = pltpu.SemaphoreType.DMA
    vmem = pl.BlockSpec(memory_space=pltpu.VMEM)
    hbm = pl.BlockSpec(memory_space=pl.ANY)
    table_shape = (places // LANES + n_slots // LANES, LANES)
    slot_rows = (n_slots // LANES, LANES)
    results = pl.pallas_call(
        functools.partial(layer_kernel, n_cols),
        out_shape=(
            pltpu.VMEM((rows, features), BF16),
            pltpu.VMEM((n_slots, part, width), BF16),
        ),
        in_specs=[vmem, hbm, hbm, hbm, hbm, hbm],
        out_specs=(vmem, vmem),
        scratch_shapes=[
            pltpu.VMEM((n_dp, n_cols, rows, features), BF16),
            pltpu.VMEM((n_dp, n_cols, rows, features), BF16),
            pltpu.VMEM((places + 1, part, width), BF16),
            pltpu.VMEM((features, 2 * hidden), BF16),
            pltpu.VMEM((hidden, features), BF16),
            pltpu.VMEM((n_dp, group_rows, 2 * hidden), BF16),
            pltpu.VMEM((n_dp, group_rows, hidden), BF16),
            pltpu.VMEM((CHUNKS, group_rows, half // CHUNKS), F32),
            pltpu.VMEM((CHUNKS, group_rows, half // CHUNKS), BF16),
            pltpu.VMEM((CHUNKS, group_rows, half // CHUNKS), BF16),
            pltpu.VMEM((CHUNKS, chips // 2, group_rows // chips, half // CHUNKS), BF16),
            pltpu.VMEM((CHUNKS, chips // 2, group_rows // chips, half // CHUNKS), BF16),
            pltpu.VMEM((CHUNKS, chips // 2, group_rows // chips, half // CHUNKS), BF16),
            pltpu.VMEM((CHUNKS, chips // 2, group_rows // chips, half // CHUNKS), BF16),
            pltpu.VMEM((rows, half), F32),
            pltpu.VMEM((rows, half), F32),
            pltpu.VMEM((2, GROUP * part, n_dp * group_rows), BF16),
            pltpu.VMEM((hidden // n_dp, n_dp * group_rows), BF16),
            pltpu.VMEM((2,) + slot_rows, jnp.int32),
            pltpu.VMEM(table_shape, jnp.int32),
            pltpu.SMEM(table_shape, jnp.int32),
            dma, dma((2,)), dma((2,)), dma,
            dma, dma((chips // 2 + 2, 2, 4)),
            dma, dma((2, 2)),
            dma, dma((chips,)), dma, dma((CHUNKS,)),
            dma, dma((CHUNKS,)), dma, dma((CHUNKS,)), dma, dma,
        ],
        compiler_params=pltpu.CompilerParams(
            collective_id=0, has_side_effects=True, vmem_limit_bytes=VMEM_LIMIT
        ),
    )(
        counts.reshape(1, 1), slot_target.reshape(slot_rows), slot_block.reshape(slot_rows), tokens, cotangent,
        block_weights.reshape(n_slots * n_dp, part, width),
    )
    return pl.pallas_call(
        out_kernel,
        out_shape=(
            jax.ShapeDtypeStruct((rows, features), BF16),
            jax.ShapeDtypeStruct((n_slots, part, width), BF16),
        ),
        in_specs=[vmem, vmem],
        out_specs=(hbm, hbm),
        scratch_shapes=[dma, dma],
        compiler_params=pltpu.CompilerParams(vmem_limit_bytes=COPY_LIMIT),
    )(*results)


def solution(mesh):
    n_dp, n_cols = mesh.shape["dp"], mesh.shape["cols"]
    paired = n_dp == 2 and n_cols == 4 * CHUNKS

    def body(*args):
        tokens, weights = args[0], args[2]
        if paired and tokens.shape[0] % 16 == 0 and weights.shape[0] % LANES == 0 and LANES * weights.shape[1] % tokens.shape[1] == 0 and weights.shape[0] // SPC % (n_cols // 4) == 0:
            return kernel_shards(n_cols, *args)
        return shards(*args)

    return jax.shard_map(
        body,
        mesh=mesh,
        in_specs=(
            P(("dp", "cols"), None),
            P(("dp", "cols"), None),
            P("cols", None, None),
            P("cols"),
            P("cols"),
            P("cols"),
        ),
        out_specs=(P(("dp", "cols"), None), P("cols", "dp", None)),
        check_vma=False,
    )
```

```python
import functools

import jax
import jax.numpy as jnp
from jax import lax
from jax.experimental import pallas as pl
from jax.experimental.pallas import tpu as pltpu
from jax.sharding import PartitionSpec as P

SPC = 32


def block_inputs(grad_rows, weights, block_select):
    partial_rows = jnp.einsum(
        "rsj,skj->rsk", grad_rows, weights, preferred_element_type=jnp.float32
    )
    summed = jnp.einsum("rsk,sb->rbk", partial_rows, block_select)
    return summed.reshape(summed.shape[0], summed.shape[1] * summed.shape[2])


def shards(tokens, cotangent, block_weights, slot_block, slot_target, counts):
    slot_total = block_weights.shape[0]
    block_width = block_weights.shape[1]
    columns = slot_total // SPC
    features = tokens.shape[1]
    block_count = features // block_width
    tokens_all, cot_all = (
        lax.all_gather(tokens, "cols", axis=0, tiled=True),
        lax.all_gather(cotangent, "cols", axis=0, tiled=True),
    )
    row_total = tokens_all.shape[0]
    live_slot = jnp.arange(slot_total) < counts[0]
    slot_kind = slot_target // columns
    places = slot_target % columns
    up_mask = (live_slot & (slot_kind < 2))[:, None].astype(jnp.float32)
    down_mask = (live_slot & (slot_kind == 2))[:, None].astype(jnp.float32)
    select_up = jax.nn.one_hot(slot_target, 2 * columns, dtype=jnp.float32) * up_mask
    select_down = jax.nn.one_hot(places, columns, dtype=jnp.float32) * down_mask
    block_select = jax.nn.one_hot(slot_block, block_count, dtype=jnp.float32)
    tokens_slots = jnp.take(
        tokens_all.reshape(row_total, block_count, block_width), slot_block, axis=1
    )
    products = jnp.einsum(
        "rsk,skj->rsj", tokens_slots, block_weights, preferred_element_type=jnp.float32
    )
    gate_up = jnp.einsum("rsj,sc->rcj", products, select_up)
    gate_pre = gate_up[:, :columns]
    up_pre = gate_up[:, columns:]
    sigmoid_gate = jax.nn.sigmoid(gate_pre)
    silu_gate = gate_pre * sigmoid_gate
    hidden = (silu_gate * up_pre).astype(jnp.bfloat16)
    cot_slots = jnp.take(cot_all.reshape(row_total, block_count, block_width), slot_block, axis=1)
    back_products = jnp.einsum(
        "rsj,skj->rsk", cot_slots, block_weights, preferred_element_type=jnp.float32
    )
    hidden_grad = jnp.einsum("rsk,sc->rck", back_products, select_down)
    gate_grad = (
        hidden_grad * up_pre * sigmoid_gate * (1.0 + gate_pre * (1.0 - sigmoid_gate))
    ).astype(jnp.bfloat16)
    up_grad = (hidden_grad * silu_gate).astype(jnp.bfloat16)
    pre_grad = jnp.concatenate([gate_grad, up_grad], axis=1)
    slot_grad = jnp.einsum(
        "rck,sc->rsk", pre_grad, select_up.astype(jnp.bfloat16), preferred_element_type=jnp.float32
    ).astype(jnp.bfloat16)
    slot_hidden = jnp.einsum(
        "rck,sc->rsk", hidden, select_down.astype(jnp.bfloat16), preferred_element_type=jnp.float32
    ).astype(jnp.bfloat16)
    weight_terms = jnp.einsum(
        "rsk,rsj->skj", tokens_slots, slot_grad, preferred_element_type=jnp.float32
    )
    weight_terms = weight_terms + jnp.einsum(
        "rsk,rsj->skj", slot_hidden, cot_slots, preferred_element_type=jnp.float32
    )
    input_terms = block_inputs(slot_grad, block_weights, block_select)
    input_sum = lax.psum_scatter(input_terms, "cols", scatter_dimension=0, tiled=True)
    input_grad = input_sum.astype(jnp.bfloat16)
    weight_sum = lax.psum_scatter(
        weight_terms.astype(jnp.bfloat16), "dp", scatter_dimension=1, tiled=True
    )
    return (input_grad, weight_sum)


MESH = pl.DeviceIdType.MESH
F32 = jnp.float32
BF16 = jnp.bfloat16
NT = (((1,), (1,)), ((), ()))
CHUNKS = 4
GROUP = 4
OUT_CUTS = 8
COPY_LIMIT = 1 << 20
VMEM_LIMIT = 60817408
LANES = 128


def layer_kernel(
    n_cols, count_ref, target_ref, block_ref, tok_ref, cot_ref, w_ref, in_ref, out_ref,
    tok, cot, blocks, wgu, wd, grads, hid, acc, sib_out, sib_in, pair_out, pair_in, line_out, line_in,
    fin_out, fin_in, lhs, hid_t, slots, table_rows, table_ref,
    w_sem, own_sem, slot_sem, table_sem, ring_send, ring_recv, sib_send, sib_recv,
    x_send, x_recv, half_send, half_recv, pair_send, pair_recv, line_send, line_recv, fin_send, fin_recv,
):
    chips = n_cols // 2
    steps = chips // 2
    rows = tok_ref.shape[0]
    group_rows = rows * n_cols
    features = tok_ref.shape[1]
    width = blocks.shape[2]
    part = blocks.shape[1]
    n_f = features // width
    hidden = wd.shape[0]
    n_h = hidden // width
    zero_at = blocks.shape[0] - 1
    pieces = width // part
    dead = w_ref.shape[0]
    table_size = zero_at // LANES
    n_slots = out_ref.shape[0]
    half = features // 2
    dp = lax.axis_index("dp")
    col = lax.axis_index("cols")
    core = col % 2
    chip = col // 2
    place = jnp.where(chip % 2 == 0, chip // 2, chips - 1 - chip // 2)

    def chip_at(p):
        p = (p + 2 * chips) % chips
        return jnp.where(p < steps, 2 * p, 2 * (chips - 1 - p) + 1)

    right = chip_at(place + 1) * 2 + core
    left = chip_at(place - 1) * 2 + core
    sibling = chip * 2 + 1 - core
    sides = ((tok_ref, tok), (cot_ref, cot))

    slot_copies = [
        pltpu.make_async_copy(ref, slots.at[a], slot_sem.at[a]) for a, ref in enumerate((target_ref, block_ref))
    ]
    for copy in slot_copies:
        copy.start()
    owns = [pltpu.make_async_copy(sides[a][0], sides[a][1].at[0, col], own_sem.at[a]) for a in range(2)]
    for own in owns:
        own.start()
    w_copy = pltpu.make_async_copy(w_ref, blocks.at[pl.ds(0, w_ref.shape[0])], w_sem)
    barrier = pltpu.get_barrier_semaphore()
    for r in range(1, chips):
        pl.semaphore_signal(barrier, inc=1, device_id=(dp, ((chip + r) % chips) * 2 + core), device_id_type=MESH)
    pl.semaphore_signal(barrier, inc=1, device_id=(dp, sibling), device_id_type=MESH)
    pl.semaphore_signal(barrier, inc=1, device_id=(1 - dp, col), device_id_type=MESH)
    pl.semaphore_wait(barrier, chips + 1)

    def piece(g, origin, a):
        at = pl.ds((a % 2) * half, half)
        return sides[a // 2][1].at[g, origin * 2 + core, :, at]

    def ring_copy(g, origin, direction, s, a):
        block = piece(g, origin, a)
        return pltpu.make_async_remote_copy(
            src_ref=block, dst_ref=block,
            send_sem=ring_send, recv_sem=ring_recv.at[g * steps + s, direction, a],
            device_id=(dp, right if direction == 0 else left), device_id_type=MESH,
        )

    def ring(g, direction, s, a):
        return ring_copy(g, chip_at(place - s if direction == 0 else place + s), direction, s, a)

    def ring_arrival(g, direction, s, a):
        return ring_copy(g, chip_at(place - 1 - s if direction == 0 else place + 1 + s), direction, s, a)

    def share_copy(g, k, a, lane):
        at = pl.ds((a % 2) * half, half)
        block = sides[a // 2][1].at[g, chip_at(place - k) * 2 + lane, :, at]
        return pltpu.make_async_remote_copy(
            src_ref=block, dst_ref=block,
            send_sem=sib_send, recv_sem=sib_recv.at[g, a // 2],
            device_id=(dp, sibling), device_id_type=MESH,
        )

    def share(g, k, a):
        return share_copy(g, k, a, core)

    def cross(k, a):
        origin = chip_at(place - k)
        return pltpu.make_async_remote_copy(
            src_ref=piece(0, origin, a), dst_ref=piece(1, origin, a),
            send_sem=x_send, recv_sem=x_recv.at[k],
            device_id=(1 - dp, col), device_id_type=MESH,
        )

    def piece_of(arr, direction, far):
        return 2 * arr + (direction if far else 1 - direction)

    def send(g, arr, s, far):
        for direction in range(2):
            ring(g, direction, s, piece_of(arr, direction, far)).start()

    def arrive(arr, s, far, forward):
        for direction in range(2):
            a = piece_of(arr, direction, far)
            ring_arrival(0, direction, s, a).wait_recv()
            if forward and s < (steps - 1 if far else steps - 2):
                ring(0, direction, s + 1, a).start()
            k = 1 + s if direction == 0 else chips - 1 - s
            share(0, k, a).start()
            if s > 1 or (s == 1 and not far):
                cross(k, a).start()

    def passed(s, far):
        arrive(1, s, far, True)

    def arrive_other(s, far):
        for direction in range(2):
            for arr in range(2):
                a = piece_of(arr, direction, far)
                ring_arrival(1, direction, s, a).wait_recv()
                if far and s == 0:
                    ring(1, direction, 1, a).start()
                share(1, 1 + s if direction == 0 else chips - 1 - s, a).start()

    def bulk(ref, send_sem, recv_sem, device):
        return pltpu.make_async_remote_copy(
            src_ref=ref, dst_ref=ref, send_sem=send_sem, recv_sem=recv_sem,
            device_id=device, device_id_type=MESH,
        )

    def all_shared(g, arr):
        bulk(sides[arr][1].at[g, pl.ds(0, chips)], sib_send, sib_recv.at[g, arr], (dp, sibling)).wait_recv()

    def cross_arrival(k, count=2):
        bulk(tok.at[1, pl.ds(0, count)], x_send, x_recv.at[k], (1 - dp, col)).wait_recv()

    def crossed(k, pieces=range(4)):
        cross_arrival(k, len(pieces) // 2)
        for a in pieces:
            share(1, k, a).start()

    for own in owns:
        own.wait()
    w_copy.start()
    send(0, 0, 0, True)
    send(0, 0, 0, False)
    send(0, 1, 0, True)
    for a in range(4):
        cross(0, a).start()
        share(0, 0, a).start()

    for copy in slot_copies:
        copy.wait()
    slot_place = slots[0] * n_f + slots[1]
    number = lax.broadcasted_iota(jnp.int32, slot_place.shape, 0) * LANES + lax.broadcasted_iota(
        jnp.int32, slot_place.shape, 1
    )
    live = number < count_ref[...]
    slot_place = jnp.where(live, slot_place, -1)
    table_rows[table_size:, :] = jnp.where(live, slot_place, zero_at)
    lane = lax.broadcasted_iota(jnp.int32, (LANES, LANES), 1)
    in_row = lax.broadcasted_iota(jnp.int32, (LANES, LANES), 0)
    columns = [
        jnp.broadcast_to(slot_place[j:j + 1], (LANES, LANES)).T for j in range(slot_place.shape[0])
    ]
    for t in range(table_size):
        row = jnp.zeros((1, LANES), jnp.int32)
        for j, column in enumerate(columns):
            hit = column == lane + t * LANES
            row = row + jnp.sum(
                jnp.where(hit, pieces * (in_row + j * LANES) - dead, 0), axis=0, keepdims=True
            )
        table_rows[t:t + 1, :] = row + dead
    table_copy = pltpu.make_async_copy(table_rows, table_ref, table_sem)
    table_copy.start()
    for at in [zero_at] + list(range(dead, dead + pieces)):
        blocks[at] = jnp.zeros((part, width), BF16)
    w_copy.wait()
    table_copy.wait()

    def spread(h, f):
        at = pl.multiple_of(f * width, width)
        hid_at = h * width
        for k in range(3):
            row, lane = divmod((k * n_h + h) * n_f, LANES)
            base = table_ref[row, lane + f]
            for piece in range(pieces):
                value = blocks[base + piece]
                if k < 2:
                    wgu[pl.ds(pl.multiple_of(at + piece * part, part), part),
                        pl.ds(k * hidden + hid_at, width)] = value
                else:
                    wd[pl.ds(hid_at + piece * part, part), pl.ds(at, width)] = value

    per_step = n_h // steps

    waiting = [(s, far) for s in range(steps) for far in (True, False) if far or s < steps - 1]
    for s in range(steps):
        if s == steps - 1:
            passed(*waiting.pop(0))
        arrive(0, s, True, True)
        if s < steps - 1:
            arrive(0, s, False, True)
        if s == 0:
            send(0, 1, 0, False)
        elif s < steps - 1:
            passed(*waiting.pop(0))
        if s < steps - 1:
            for u in range(2 * steps * s // (steps - 1), 2 * steps * (s + 1) // (steps - 1)):
                @pl.loop(u % 2 * n_f // 2, (u % 2 + 1) * n_f // 2, unroll=4)
                def _(f):
                    for j in range(per_step):
                        spread(u // 2 * per_step + j, f)

    all_shared(0, 0)
    span = hidden // steps

    def before(g, n):
        at = pl.multiple_of(n * span, span)
        x = tok[g].reshape(group_rows, features)
        gate = jnp.dot(x, wgu[:, pl.ds(at, span)], preferred_element_type=F32)
        up = jnp.dot(x, wgu[:, pl.ds(pl.multiple_of(hidden + at, span), span)], preferred_element_type=F32)
        return gate, up

    def after(g, n, gate, up):
        at = pl.multiple_of(n * span, span)
        back = lax.dot_general(
            cot[g].reshape(group_rows, features), wd[pl.ds(at, span), :], NT, preferred_element_type=F32
        )
        sig = jax.nn.sigmoid(gate)
        silu = gate * sig
        hid[g, :, pl.ds(at, span)] = (silu * up).astype(BF16)
        grads[g, :, pl.ds(at, span)] = (back * up * sig * (1.0 + gate * (1.0 - sig))).astype(BF16)
        grads[g, :, pl.ds(pl.multiple_of(hidden + at, span), span)] = (back * silu).astype(BF16)

    def take_part(block):
        out = block[:part]
        for i in range(1, width // part):
            out = jnp.where(dp == i, block[i * part:(i + 1) * part], out)
        return out

    def turn_hidden(g):
        for h in range(n_h):
            hid_t[pl.ds(h * part, part), pl.ds(g * group_rows, group_rows)] = take_part(
                hid[g, :, pl.ds(h * width, width)].T
            )

    for s in range(steps):
        gate, up = before(0, s)
        sig = jax.nn.sigmoid(gate)
        silu = gate * sig
        hid[0, :, s * span:(s + 1) * span] = (silu * up).astype(BF16)
        acc[s, :, :span] = up * sig * (1.0 + gate * (1.0 - sig))
        acc[s, :, span:] = silu
        passed(*waiting.pop(0))
        if s == steps - 3:
            cross_arrival(0)
            for far in (True, False):
                for arr in range(2):
                    send(1, arr, 0, far)
            for a in range(4):
                share(1, 0, a).start()

    turn_hidden(0)
    all_shared(0, 1)

    for s in range(steps):
        at = s * span
        back = lax.dot_general(
            cot[0].reshape(group_rows, features), wd[at:at + span, :], NT, preferred_element_type=F32
        )
        grads[0, :, at:at + span] = (back * acc[s, :, :span]).astype(BF16)
        grads[0, :, hidden + at:hidden + at + span] = (back * acc[s, :, span:]).astype(BF16)

    crossed(2, (1, 3))
    crossed(chips - 2, (0, 2))
    arrive_other(0, True)

    chunk = half // CHUNKS
    chip_rows = group_rows // chips

    def terms(at):
        return lax.dot_general(grads[0], wgu[pl.ds(at, chunk), :], NT, preferred_element_type=F32)

    def to_sibling(i):
        return pltpu.make_async_remote_copy(
            src_ref=sib_out.at[i], dst_ref=sib_in.at[i], send_sem=half_send, recv_sem=half_recv.at[i],
            device_id=(dp, sibling), device_id_type=MESH,
        )

    lines = chips // 2
    line, side = chip // 2, chip % 2

    def rows_of(zz, yy):
        return pl.ds(pl.multiple_of((2 * zz + yy) * chip_rows, chip_rows), chip_rows)

    def to_partner(i):
        return pltpu.make_async_remote_copy(
            src_ref=pair_out.at[i], dst_ref=pair_in.at[i], send_sem=pair_send, recv_sem=pair_recv.at[i],
            device_id=(dp, (2 * line + 1 - side) * 2 + core), device_id_type=MESH,
        )

    def along_line(r, i):
        other = (line + r) % lines
        return pltpu.make_async_remote_copy(
            src_ref=line_out.at[i, other], dst_ref=line_in.at[i, r],
            send_sem=line_send, recv_sem=line_recv.at[i],
            device_id=(dp, (2 * other + side) * 2 + core), device_id_type=MESH,
        )

    def pair_add(i):
        for zz in range(lines):
            at = rows_of(zz, 1 - side)
            pair_out[i, zz] = (acc[i, at, :] + sib_in[i, at, :].astype(F32)).astype(BF16)
        to_partner(i).start()
        for zz in range(lines):
            at = rows_of(zz, side)
            acc[i, at, :] = acc[i, at, :] + sib_in[i, at, :].astype(F32)

    def pair_sum(i):
        to_sibling(i).wait_recv()
        pair_add(i)

    def line_sum(i):
        to_partner(i).wait_recv()

        @pl.loop(0, lines)
        def _(zz):
            at = rows_of(zz, side)
            total = acc[i, at, :] + pair_in[i, zz].astype(F32)
            acc[i, at, :] = total
            line_out[i, zz] = total.astype(BF16)

        for r in range(1, lines):
            along_line(r, i).start()

    for i in range(CHUNKS):
        at = i * chunk
        sib_out[i] = terms(pl.multiple_of((1 - core) * half + at, chunk)).astype(BF16)
        to_sibling(i).start()
        if i > 0:
            to_sibling(i - 1).wait_recv()
        acc[i] = terms(pl.multiple_of(core * half + at, chunk))
        if i > 0:
            pair_add(i - 1)
        if i == 0:
            arrive_other(0, False)
        if i == CHUNKS - 3:
            crossed(3)
            crossed(chips - 3)
        if i == CHUNKS - 2:
            arrive_other(1, True)
            for k in range(4, chips - 3):
                crossed(k)

    all_shared(1, 0)
    all_shared(1, 1)

    @pl.loop(0, steps)
    def _(s):
        gate, up = before(1, s)
        after(1, s, gate, up)

        @pl.when(s == 0)
        def _():
            pair_sum(CHUNKS - 1)

        @pl.when(s != CHUNKS - 2)
        def _():
            line_sum(jnp.minimum(s, CHUNKS - 2))

    turn_hidden(1)
    four = GROUP
    mine = rows_of(line, side)
    early = half - chunk

    def fin(j):
        at = pl.ds(0, early) if j == 0 else pl.ds(early, chunk)
        return pltpu.make_async_remote_copy(
            src_ref=fin_out.at[:, at], dst_ref=fin_in.at[:, at],
            send_sem=fin_send.at[j], recv_sem=fin_recv.at[j],
            device_id=(dp, sibling), device_id_type=MESH,
        )

    def final_sum(i):
        total = acc[i, mine, :]
        bulk(line_in.at[i, pl.ds(1, lines - 1)], line_send, line_recv.at[i], (dp, sibling)).wait_recv()
        for r in range(1, lines):
            total = total + line_in[i, r].astype(F32)
        low, high = total[:rows], total[rows:]
        at = pl.multiple_of(i * chunk, chunk)
        fin_out[:, pl.ds(at, chunk)] = jnp.where(core == 0, high, low)
        in_ref[:, pl.ds(pl.multiple_of(core * half + at, chunk), chunk)] = jnp.where(
            core == 0, low, high
        ).astype(BF16)

    tiles = n_f // four

    def prepare(i, slot):
        at = jnp.minimum(i, tiles - 1) * four * width
        for g in range(2):
            for b in range(four):
                piece = tok[g, :, :, pl.ds(pl.multiple_of(at + b * width, width), width)]
                lhs[slot, pl.ds(b * part, part), pl.ds(g * group_rows, group_rows)] = take_part(
                    piece.reshape(group_rows, width).T
                )

    def tile_grads(i, slot):
        for n in range(2 * n_h // 4):
            cut = slice(n * 4 * width, (n + 1) * 4 * width)
            out = jnp.dot(
                lhs[slot], grads[:, :, cut].reshape(2 * group_rows, 4 * width), preferred_element_type=F32
            ).astype(BF16)
            for h in range(4):
                for b in range(four):
                    blocks[(n * 4 + h) * n_f + i * four + b] = out[
                        b * part:(b + 1) * part, h * width:(h + 1) * width
                    ]
            if n == 0:
                prepare(i + 1, 1 - slot)
        c = cot[:, :, :, pl.ds(pl.multiple_of(i * four * width, width), four * width)]
        out = jnp.dot(
            hid_t[...], c.reshape(2 * group_rows, four * width), preferred_element_type=F32
        ).astype(BF16)
        for h in range(n_h):
            for b in range(four):
                blocks[(2 * n_h + h) * n_f + i * four + b] = out[
                    h * part:(h + 1) * part, b * width:(b + 1) * width
                ]

    prepare(0, 0)

    @pl.loop(0, tiles // 2)
    def _(p):
        tile_grads(2 * p, 0)

        @pl.when(p == 0)
        def _():
            line_sum(CHUNKS - 1)

        @pl.when(p == tiles // 2 - 1)
        def _():
            @pl.loop(0, CHUNKS - 1)
            def _(n):
                final_sum(n)

            fin(0).start()

        tile_grads(2 * p + 1, 1)

    final_sum(CHUNKS - 1)
    fin(1).start()

    for r in range(n_slots // LANES):
        @pl.loop(0, LANES, unroll=32)
        def _(j):
            out_ref[r * LANES + j] = blocks[table_ref[table_size + r, j]]

    bulk(sib_out, half_send, half_recv.at[0], (dp, sibling)).wait_send()
    bulk(pair_out, pair_send, pair_recv.at[0], (dp, sibling)).wait_send()
    bulk(line_out.at[:, pl.ds(1, lines - 1)], line_send, line_recv.at[0], (dp, sibling)).wait_send()
    bulk(tok, sib_send, sib_recv.at[0, 0], (dp, sibling)).wait_send()
    bulk(tok.at[0, pl.ds(0, 2 * chips - 6)], x_send, x_recv.at[0], (1 - dp, col)).wait_send()
    bulk(tok.at[:, pl.ds(0, chips + 2)], ring_send, ring_recv.at[0, 0, 0], (dp, right)).wait_send()
    for j in range(2):
        fin(j).wait()
    in_ref[:, pl.ds(pl.multiple_of((1 - core) * half, half), half)] = fin_in[...].astype(BF16)


def out_kernel(in_ref, wg_ref, in_out, wg_out, in_sem, wg_sem):
    per_cut = wg_ref.shape[0] // OUT_CUTS
    first = pltpu.make_async_copy(in_ref, in_out, in_sem)
    first.start()
    for c in range(OUT_CUTS):
        at = pl.ds(c * per_cut, per_cut)
        pltpu.make_async_copy(wg_ref.at[at], wg_out.at[at], wg_sem).start()
    first.wait()
    pltpu.make_async_copy(wg_ref, wg_out, wg_sem).wait()


def kernel_shards(n_cols, tokens, cotangent, block_weights, slot_block, slot_target, counts):
    n_slots, width = block_weights.shape[:2]
    n_dp = 2
    part = width // n_dp
    rows, features = tokens.shape
    n_f = features // width
    hidden_blocks = n_slots // SPC
    hidden = hidden_blocks * width
    places = 3 * hidden_blocks * n_f
    chips = n_cols // 2
    group_rows = rows * n_cols
    half = features // 2
    dma = pltpu.SemaphoreType.DMA
    vmem = pl.BlockSpec(memory_space=pltpu.VMEM)
    hbm = pl.BlockSpec(memory_space=pl.ANY)
    table_shape = (places // LANES + n_slots // LANES, LANES)
    slot_rows = (n_slots // LANES, LANES)
    results = pl.pallas_call(
        functools.partial(layer_kernel, n_cols),
        out_shape=(
            pltpu.VMEM((rows, features), BF16),
            pltpu.VMEM((n_slots, part, width), BF16),
        ),
        in_specs=[vmem, hbm, hbm, hbm, hbm, hbm],
        out_specs=(vmem, vmem),
        scratch_shapes=[
            pltpu.VMEM((n_dp, n_cols, rows, features), BF16),
            pltpu.VMEM((n_dp, n_cols, rows, features), BF16),
            pltpu.VMEM((places + 1, part, width), BF16),
            pltpu.VMEM((features, 2 * hidden), BF16),
            pltpu.VMEM((hidden, features), BF16),
            pltpu.VMEM((n_dp, group_rows, 2 * hidden), BF16),
            pltpu.VMEM((n_dp, group_rows, hidden), BF16),
            pltpu.VMEM((CHUNKS, group_rows, half // CHUNKS), F32),
            pltpu.VMEM((CHUNKS, group_rows, half // CHUNKS), BF16),
            pltpu.VMEM((CHUNKS, group_rows, half // CHUNKS), BF16),
            pltpu.VMEM((CHUNKS, chips // 2, group_rows // chips, half // CHUNKS), BF16),
            pltpu.VMEM((CHUNKS, chips // 2, group_rows // chips, half // CHUNKS), BF16),
            pltpu.VMEM((CHUNKS, chips // 2, group_rows // chips, half // CHUNKS), BF16),
            pltpu.VMEM((CHUNKS, chips // 2, group_rows // chips, half // CHUNKS), BF16),
            pltpu.VMEM((rows, half), F32),
            pltpu.VMEM((rows, half), F32),
            pltpu.VMEM((2, GROUP * part, n_dp * group_rows), BF16),
            pltpu.VMEM((hidden // n_dp, n_dp * group_rows), BF16),
            pltpu.VMEM((2,) + slot_rows, jnp.int32),
            pltpu.VMEM(table_shape, jnp.int32),
            pltpu.SMEM(table_shape, jnp.int32),
            dma, dma((2,)), dma((2,)), dma,
            dma, dma((chips // 2 + 2, 2, 4)),
            dma, dma((2, 2)),
            dma, dma((chips,)), dma, dma((CHUNKS,)),
            dma, dma((CHUNKS,)), dma, dma((CHUNKS,)), dma((2,)), dma((2,)),
        ],
        compiler_params=pltpu.CompilerParams(
            collective_id=0, has_side_effects=True, vmem_limit_bytes=VMEM_LIMIT
        ),
    )(
        counts.reshape(1, 1), slot_target.reshape(slot_rows), slot_block.reshape(slot_rows), tokens, cotangent,
        block_weights.reshape(n_slots * n_dp, part, width),
    )
    return pl.pallas_call(
        out_kernel,
        out_shape=(
            jax.ShapeDtypeStruct((rows, features), BF16),
            jax.ShapeDtypeStruct((n_slots, part, width), BF16),
        ),
        in_specs=[vmem, vmem],
        out_specs=(hbm, hbm),
        scratch_shapes=[dma, dma],
        compiler_params=pltpu.CompilerParams(vmem_limit_bytes=COPY_LIMIT),
    )(*results)


def solution(mesh):
    n_dp, n_cols = mesh.shape["dp"], mesh.shape["cols"]
    paired = n_dp == 2 and n_cols == 4 * CHUNKS

    def body(*args):
        tokens, weights = args[0], args[2]
        if paired and tokens.shape[0] % 16 == 0 and weights.shape[0] % LANES == 0 and LANES * weights.shape[1] % tokens.shape[1] == 0 and weights.shape[0] // SPC % (n_cols // 4) == 0:
            return kernel_shards(n_cols, *args)
        return shards(*args)

    return jax.shard_map(
        body,
        mesh=mesh,
        in_specs=(
            P(("dp", "cols"), None),
            P(("dp", "cols"), None),
            P("cols", None, None),
            P("cols"),
            P("cols"),
            P("cols"),
        ),
        out_specs=(P(("dp", "cols"), None), P("cols", "dp", None)),
        check_vma=False,
    )
```
